32 devices in a mesh: edata: 4 (over z), expert: 8 (over y, x, core).
Axes of the slice: x: 2, y: 2, z: 4, core: 2. Of those that a mesh axis runs over, the one named last changes fastest.
Arguments:
- tokens: bfloat16 [1024, 4096], P('expert', 'edata'), may hold values from -6 to 6
- grad_out: bfloat16 [1024, 4096], P('expert', 'edata'), may hold values from -6 to 6
- expert_ids: int32 [1024, 8], P('expert'), may hold values from 0 to 15, all different within a row; in each aligned block of 128 rows (0 to 127, 128 to 255, ...) at most 80 rows name the same one
- route_prob: float32 [1024, 8], P('expert'), may hold values from 0.05 to 0.5
- w_gate: bfloat16 [16, 1024, 4096], P('expert', 'edata'), may hold values from -0.09375 to 0.09375
- w_up: bfloat16 [16, 1024, 4096], P('expert', 'edata'), may hold values from -0.09375 to 0.09375
- w_down: bfloat16 [16, 1024, 4096], P('expert', 'edata'), may hold values from -0.1875 to 0.1875
Outputs:
- grad_tokens: bfloat16 [1024, 4096], P('expert', 'edata')
- grad_gate: bfloat16 [16, 1024, 4096], P('expert', 'edata')
- grad_up: bfloat16 [16, 1024, 4096], P('expert', 'edata')
- grad_down: bfloat16 [16, 1024, 4096], P('expert', 'edata')
The draws below stay inside these ranges and needn't reach their ends.
Inputs may be any that keep to these rules, and one draw needn't show every extreme that they name: `expert_ids`: each token names 8 different experts. Among the tokens of one aligned block of 128 no expert is named more than 80 times, and in every draw some expert is named exactly 80 times in some block.
All inputs are finite; a program needn't handle non-finite values.
Results may differ from the reference program's by a relative error of at most 0.012.
Values may be sent and summed in bfloat16 or wider, within the bound.
A program may use at most 192 MiB of HBM per device.

```python
import math
import jax
import jax.numpy as jnp
import numpy as np
from jax import lax

D = 4096
FF = 1024
TOP = 8
TOK_DEV = 128
EXPERTS = 16
TOKENS = 1024
CAP = 80
N_EDATA = 4
N_EXPERT = 8


def block_levels(own_key, extent, split, low, largest):
    loudness, own = 1.0, jax.random.fold_in(own_key, 6)
    for dim, blocks in split:
        heights = jnp.exp(jax.random.uniform(jax.random.fold_in(own, dim), (blocks,), jnp.float32, low / len(split), largest / len(split)))
        loudness = loudness * jnp.repeat(heights, extent[dim] // blocks).reshape([-1 if axis == dim else 1 for axis in range(len(extent))])
    return loudness


def routed_block(key, own, number, rows, count, top, most, skew):
    ranking = jax.random.permutation(key, count)
    packed, common = shares(count, rows * top, most, skew, True), shares(count, rows * top, most, skew, False)
    places = jnp.arange(count)

    def named(tallies, offset_by):
        used = int((tallies > 0).sum())
        fixed = max(1, used // 4)
        shifted = fixed + (places - fixed + offset_by * (used - fixed)) % max(1, count - fixed)
        return jnp.zeros((count,), jnp.int32).at[ranking[jnp.where(places < fixed, places, shifted)]].set(jnp.asarray(tallies, jnp.int32))

    tallies = jnp.where(number % 4 == 0, named(packed, number // 4), named(common, number - number // 4 - 1))
    mixed = jax.random.permutation(jax.random.fold_in(own, 3), count)
    source_of, sink = mixed[0:count // 2 * 2:2], mixed[1:count // 2 * 2:2]
    room = jnp.minimum(tallies[source_of] - 1, most - tallies[sink]) // 2
    room = jnp.where((source_of == ranking[0]) | (sink == ranking[0]) | (tallies[sink] == 0), 0, jnp.maximum(room, 0))
    shifted = jax.random.randint(jax.random.fold_in(own, 4), (count // 2,), 0, 1 << 20) % (room + 1)
    tallies = tallies.at[source_of].add(-shifted).at[sink].add(shifted)
    members = jnp.searchsorted(jnp.cumsum(tallies), jnp.arange(rows * top), side="right").astype(jnp.int32)
    grid = members.reshape(top, rows).T
    grid = grid[jax.random.permutation(jax.random.fold_in(own, 1), rows)]
    offset_by = jax.random.randint(jax.random.fold_in(own, 2), (rows, 1), 0, top)
    return jnp.take_along_axis(grid, (jnp.arange(top)[None, :] + offset_by) % top, axis=1)


def shares(number_of, total, most, skew, full):
    loads = [(1 << 20) // math.isqrt(grade ** skew) + 1 for grade in range(1, number_of + 1)]
    largest = most if full else min(most, max(-(-total // number_of), total * loads[0] // sum(loads)))
    least = 1 if total - largest >= number_of - 1 else 0
    given, rest = [largest] + [least] * (number_of - 1), total - largest - least * (number_of - 1)
    while rest > 0:
        candidates = [i for i in range(1, number_of) if given[i] < largest] or [i for i in range(1, number_of) if given[i] < most]
        pool, left = sum([loads[i] for i in candidates]), rest
        for i in candidates:
            extra = min(most - given[i], max(1, left * loads[i] // pool), rest)
            given[i] = given[i] + extra
            rest = rest - extra
    return np.array(given)


def gaussian(rng, extent, spread, reach, pieces=(), kind=jnp.bfloat16):
    drawn = jax.random.normal(rng, extent, jnp.float32) * spread
    if len(pieces) > 0:
        drawn = block_levels(rng, extent, pieces, -0.22, 0.18) * drawn
    return jnp.clip(drawn, min=-reach, max=reach).astype(kind)


def setup_inputs(seed: int = 0) -> dict:
    key_of = jax.random.split(jax.random.key(seed), 8)
    tokens = gaussian(key_of[0], (TOKENS, D), 1.0, 6.0, ((0, 8), (1, 4)))
    grad_out = gaussian(key_of[1], (TOKENS, D), 1.0, 6.0, ((0, 8), (1, 4)))
    expert_ids_keys = jax.random.split(jax.random.fold_in(key_of[2], 1), TOKENS // TOK_DEV)
    expert_ids_turns = jax.random.permutation(jax.random.fold_in(key_of[2], 3), TOKENS // TOK_DEV)
    expert_ids = jax.vmap(lambda own, number: routed_block(jax.random.fold_in(key_of[2], 2), own, number, TOK_DEV, EXPERTS, TOP, CAP, 1))(expert_ids_keys, expert_ids_turns).reshape((TOKENS, TOP))
    route_prob = jnp.clip(jnp.exp(math.log(0.5) - 2.3025851 * jax.random.uniform(key_of[3], (TOKENS, TOP), jnp.float32) ** block_levels(key_of[3], (TOKENS, TOP), ((0, 8),), -0.2, 0.2)), 0.05, 0.5)
    w_gate = gaussian(key_of[4], (EXPERTS, FF, D), D ** -0.5, 0.09375, ((0, 8), (1, 4)))
    w_up = gaussian(key_of[5], (EXPERTS, FF, D), D ** -0.5, 0.09375, ((0, 8), (1, 4)))
    w_down = gaussian(key_of[6], (EXPERTS, FF, D), FF ** -0.5, 0.1875, ((0, 8), (1, 4)))
    return dict(tokens=tokens, grad_out=grad_out, expert_ids=expert_ids, route_prob=route_prob, w_gate=w_gate, w_up=w_up, w_down=w_down)


def reference(tokens, grad_out, expert_ids, route_prob, w_gate, w_up, w_down):
    pair_count = TOK_DEV * TOP
    blocks = expert_ids.reshape(N_EXPERT, pair_count)
    onehot = (blocks[:, :, None] == jnp.arange(EXPERTS, dtype=jnp.int32)[None, None, :]).astype(jnp.int32)
    slots = jnp.sum((jnp.cumsum(onehot, 1) - onehot) * onehot, 2).astype(jnp.int32)
    source = jnp.broadcast_to(jnp.arange(N_EXPERT, dtype=jnp.int32)[:, None], (N_EXPERT, pair_count))
    global_pair = source * pair_count + jnp.arange(pair_count, dtype=jnp.int32)[None, :]
    table = jnp.full((EXPERTS, N_EXPERT, CAP), TOKENS * TOP, jnp.int32)
    table = table.at[blocks, source, slots].set(global_pair)
    x_padded = jnp.concatenate([tokens, jnp.zeros((1, D), jnp.bfloat16)], 0)
    dy_padded = jnp.concatenate([grad_out, jnp.zeros((1, D), jnp.bfloat16)], 0)
    prob_padded = jnp.concatenate([route_prob.reshape(-1), jnp.zeros((1,), jnp.float32)], 0)
    group = FF // N_EDATA

    def one_expert(carry, inputs):
        rows, weight_gate, weight_up, weight_down = inputs
        rows = rows.reshape(-1)
        token_of = (rows // TOP).astype(jnp.int32)
        xs = x_padded[token_of]
        ds = (prob_padded[rows][:, None] * dy_padded[token_of].astype(jnp.float32)).astype(jnp.bfloat16)
        gate_value = jnp.dot(xs, weight_gate.T, preferred_element_type=jnp.float32)
        up_value = jnp.dot(xs, weight_up.T, preferred_element_type=jnp.float32)
        sigma = jax.nn.sigmoid(gate_value)
        active = gate_value * sigma
        hidden = (active * up_value).astype(jnp.bfloat16)
        back = jnp.dot(ds, weight_down.T, preferred_element_type=jnp.float32)
        gate_grad = (back * up_value * sigma * (1.0 + gate_value * (1.0 - sigma))).astype(jnp.bfloat16)
        up_grad = (back * active).astype(jnp.bfloat16)
        grad_g = jnp.dot(gate_grad.T, xs, preferred_element_type=jnp.float32).astype(jnp.bfloat16)
        grad_u = jnp.dot(up_grad.T, xs, preferred_element_type=jnp.float32).astype(jnp.bfloat16)
        grad_d = jnp.dot(hidden.T, ds, preferred_element_type=jnp.float32).astype(jnp.bfloat16)
        total = jnp.zeros((rows.shape[0], D), jnp.float32)
        for index in range(N_EDATA):
            lower = index * group
            upper = lower + group
            part = jnp.dot(gate_grad[:, lower:upper], weight_gate[lower:upper, :], preferred_element_type=jnp.float32)
            part = part + jnp.dot(up_grad[:, lower:upper], weight_up[lower:upper, :], preferred_element_type=jnp.float32)
            part = lax.optimization_barrier(part.astype(jnp.bfloat16))
            total = total + part.astype(jnp.float32)
        carry = carry.at[token_of].add(total)
        return carry, (grad_g, grad_u, grad_d)

    start = jnp.zeros((TOKENS + 1, D), jnp.float32)
    final, grads = lax.scan(one_expert, start, (table, w_gate, w_up, w_down))
    grad_tokens = final[:TOKENS].astype(jnp.bfloat16)
    return (grad_tokens, grads[0], grads[1], grads[2])
```

```python
import jax
import jax.numpy as jnp
from jax import lax
from jax.experimental import pallas as pl
from jax.experimental.pallas import tpu as pltpu
from jax.sharding import PartitionSpec as P

MESH = pl.DeviceIdType.MESH
BF16 = jnp.bfloat16
F32 = jnp.float32


def ranks(onehot):
    pair_count = onehot.shape[-2]
    row = lax.broadcasted_iota(jnp.int32, (pair_count, pair_count), 0)
    col = lax.broadcasted_iota(jnp.int32, (pair_count, pair_count), 1)
    tri = (col < row).astype(jnp.bfloat16)
    earlier = jnp.einsum(
        "pq,...qe->...pe", tri, onehot.astype(jnp.bfloat16), preferred_element_type=jnp.float32
    )
    return earlier.astype(jnp.int32)


def slots_body(tokens, grad_out, expert_ids, route_prob, w_gate, w_up, w_down):
    token_count, top_count = expert_ids.shape
    local_experts = w_gate.shape[0]
    expert_devices = lax.axis_size("expert")
    me = lax.axis_index("expert")
    experts_all = expert_devices * local_experts
    capacity = token_count * top_count * 5 // (4 * experts_all)
    pair_count = token_count * top_count
    cap_iota = jnp.arange(capacity, dtype=jnp.int32)

    routing = jnp.stack([expert_ids.astype(jnp.float32), route_prob])
    routing = lax.all_gather(routing, "expert", axis=1, tiled=False)
    all_ids, all_prob = routing[0].astype(jnp.int32), routing[1]
    mine = me * local_experts + jnp.arange(local_experts, dtype=jnp.int32)
    named = all_ids.reshape(expert_devices, pair_count)[:, :, None] == mine
    rank = ranks(named)
    hit = named[..., None] & (rank[..., None] == cap_iota)
    hit = hit.reshape(expert_devices, token_count, top_count, local_experts, capacity)
    pick = jnp.sum(hit.astype(jnp.int32), 2).astype(jnp.bfloat16)
    prob_of = jnp.sum(jnp.where(hit, all_prob[:, :, :, None, None], 0.0), (1, 2))

    both = lax.all_gather(jnp.stack([tokens, grad_out]), "edata", axis=2, tiled=True)
    both = lax.all_gather(both, "expert", axis=1, tiled=False)
    all_x, all_dy = both[0], both[1]
    slot_x = jnp.einsum(
        "stxc,std->sxcd", pick, all_x, preferred_element_type=jnp.float32
    ).astype(jnp.bfloat16)
    slot_dy = jnp.einsum("stxc,std->sxcd", pick, all_dy, preferred_element_type=jnp.float32)
    slot_dy = (prob_of[..., None] * slot_dy).astype(jnp.bfloat16)

    gate_value = jnp.einsum("sxcd,xfd->sxcf", slot_x, w_gate, preferred_element_type=jnp.float32)
    up_value = jnp.einsum("sxcd,xfd->sxcf", slot_x, w_up, preferred_element_type=jnp.float32)
    sigma = jax.nn.sigmoid(gate_value)
    active = gate_value * sigma
    hidden = (active * up_value).astype(jnp.bfloat16)
    back = jnp.einsum("sxcd,xfd->sxcf", slot_dy, w_down, preferred_element_type=jnp.float32)
    gate_grad = (back * up_value * sigma * (1.0 + gate_value * (1.0 - sigma))).astype(jnp.bfloat16)
    up_grad = (back * active).astype(jnp.bfloat16)
    grad_gate = jnp.einsum(
        "sxcf,sxcd->xfd", gate_grad, slot_x, preferred_element_type=jnp.float32
    ).astype(jnp.bfloat16)
    grad_up = jnp.einsum(
        "sxcf,sxcd->xfd", up_grad, slot_x, preferred_element_type=jnp.float32
    ).astype(jnp.bfloat16)
    grad_down = jnp.einsum(
        "sxcf,sxcd->xfd", hidden, slot_dy, preferred_element_type=jnp.float32
    ).astype(jnp.bfloat16)
    partial_value = jnp.einsum(
        "sxcf,xfd->sxcd", gate_grad, w_gate, preferred_element_type=jnp.float32
    )
    partial_value = partial_value + jnp.einsum(
        "sxcf,xfd->sxcd", up_grad, w_up, preferred_element_type=jnp.float32
    )
    partial_value = partial_value.astype(jnp.bfloat16)
    returned = lax.all_to_all(
        partial_value.reshape(expert_devices, local_experts * capacity, -1),
        "expert",
        split_axis=0,
        concat_axis=0,
        tiled=True,
    )
    width = returned.shape[-1]

    own = expert_ids.reshape(pair_count, 1) == jnp.arange(experts_all, dtype=jnp.int32)
    slot = jnp.sum(jnp.where(own, ranks(own), 0), 1)
    back_hit = own[:, :, None] & (slot[:, None, None] == cap_iota)
    gather_back = jnp.sum(
        back_hit.reshape(token_count, top_count, experts_all * capacity).astype(jnp.int32), 1
    ).astype(jnp.bfloat16)
    per_token = jnp.einsum(
        "tq,qd->td",
        gather_back,
        returned.reshape(experts_all * capacity, width),
        preferred_element_type=jnp.float32,
    )
    grad_tokens = lax.psum_scatter(per_token, "edata", scatter_dimension=1, tiled=True).astype(
        jnp.bfloat16
    )
    return (grad_tokens, grad_gate, grad_up, grad_down)


def dense_kernel(
    tokens_ref, dy_ref, ids_ref, prob_ref, wg_ref, wu_ref, wd_ref,
    gt_ref, gw_ref,
    act, wv, acc, gh, gT, Q, RC, RX, RY, RZ, pt, stage, outv,
    w_sem, own_sem, pt_s, pt_r, up_s, dn_s, col_r, gx_s, gx_r, gy_s, gy_r,
    hx_s, hx_r, hy_s, hy_r, gc_s, gc_r, rc_s, rc_r, rx_s, rx_r, ry_s, ry_r,
    rz_s, rz_r, wg_sem, out_sem,
):
    T, FC = tokens_ref.shape
    H = wg_ref.shape[1]
    half = T // 2
    z = lax.axis_index("edata")
    p = lax.axis_index("expert")
    c = lax.rem(p, 2)
    x = lax.rem(lax.div(p, 2), 2)
    y = lax.div(p, 4)

    def q_of(qi):
        a, b = qi % 2, qi // 2
        if not isinstance(qi, int):
            a, b = lax.rem(qi, 2), lax.div(qi, 2)
        return (y + b * (1 - 2 * y)) * 2 + (x + a * (1 - 2 * x))

    def block_of(qi):
        return q_of(qi) * 2 + c

    px, py, pd, pc = block_of(1), block_of(2), block_of(3), q_of(0) * 2 + 1 - c
    dev_x, dev_y, dev_c = (z, px), (z, py), (z, pc)

    def rows(block, first=0, size=T):
        return pl.ds(pl.multiple_of(block * T + first, half), size)

    def cols(q):
        return pl.ds(pl.multiple_of(q * 2 * T, 2 * T), 2 * T)

    def feature_of(j):
        hi = lax.div(z, 2)
        zz = hi * (3 - z) + (1 - hi) * z
        near = jnp.where(j == 0, zz, 1 - zz)
        g = jnp.where(j < 2, near, j)
        return hi * (3 - g) + (1 - hi) * g

    def send(src, dst, s_sem, r_sem, dev):
        pltpu.make_async_remote_copy(
            src_ref=src, dst_ref=dst, send_sem=s_sem, recv_sem=r_sem,
            device_id=dev, device_id_type=MESH,
        ).start()

    def got(dst, sem):
        pltpu.make_async_copy(dst, dst, sem).wait()

    wrefs = (wg_ref, wu_ref, wd_ref)

    def w_copy(r, f):
        return pltpu.make_async_copy(
            wrefs[r // 2].at[r % 2, :, pl.ds(f * FC, FC)],
            wv.at[f, pl.ds(r * H, H), :],
            w_sem.at[r, f],
        )

    own_x = pltpu.make_async_copy(tokens_ref, act.at[0, z, rows(p)], own_sem.at[0])
    own_dy = pltpu.make_async_copy(dy_ref, act.at[1, z, rows(p)], own_sem.at[1])
    own_x.start()
    own_dy.start()
    for r in range(6):
        for f in range(4):
            w_copy(r, f).start()

    lane = lax.broadcasted_iota(jnp.int32, (T, 128), 1)
    dense = jnp.zeros((T, 128), F32)
    for k in range(ids_ref.shape[1]):
        dense = dense + jnp.where(lane == ids_ref[:, k : k + 1], prob_ref[:, k : k + 1], 0.0)
    pt[p] = dense.T[: pt.shape[1]]

    bar = pltpu.get_barrier_semaphore()
    for d in range(1, 8):
        pl.semaphore_signal(bar, inc=1, device_id=(z, lax.rem(p + d, 8)), device_id_type=MESH)
    for d in range(1, 4):
        pl.semaphore_signal(bar, inc=1, device_id=(lax.rem(z + d, 4), p), device_id_type=MESH)
    pl.semaphore_wait(bar, 10)

    own_x.wait()
    own_dy.wait()

    def col_block(s):
        arr, j = lax.div(s, 4), lax.rem(s, 4)
        f = feature_of(j)
        i = arr * 4 + f
        ref = act.at[arr, f, rows(p)]

        @pl.when(j > 0)
        def _():
            got(ref, col_r.at[i])

        @pl.when((f <= z) & (z < 3))
        def _():
            send(ref, ref, up_s.at[i], col_r.at[i], (z + 1, p))

        @pl.when((f >= z) & (z > 0))
        def _():
            send(ref, ref, dn_s.at[i], col_r.at[i], (z - 1, p))

        send(ref, ref, gx_s.at[s], gx_r.at[s], dev_x)
        send(ref, ref, gy_s.at[s], gy_r.at[s], dev_y)
        send(ref, ref, gc_s.at[0, s], gc_r.at[0, s], dev_c)

    def near_blocks(s):
        arr, f = lax.div(s, 4), feature_of(lax.rem(s, 4))
        rx = act.at[arr, f, rows(px)]
        got(rx, gx_r.at[s])
        hy = act.at[arr, f, rows(px, 0, half)]
        send(hy, hy, hy_s.at[s], hy_r.at[s], dev_y)
        send(rx, rx, gc_s.at[1, s], gc_r.at[1, s], dev_c)
        ry = act.at[arr, f, rows(py)]
        got(ry, gy_r.at[s])
        hx = act.at[arr, f, rows(py, half, half)]
        send(hx, hx, hx_s.at[s], hx_r.at[s], dev_x)
        send(ry, ry, gc_s.at[2, s], gc_r.at[2, s], dev_c)

    def far_block(s):
        arr, f = lax.div(s, 4), feature_of(lax.rem(s, 4))
        got(act.at[arr, f, rows(pd, 0, half)], hy_r.at[s])
        got(act.at[arr, f, rows(pd, half, half)], hx_r.at[s])
        ref = act.at[arr, f, rows(pd)]
        send(ref, ref, gc_s.at[3, s], gc_r.at[3, s], dev_c)

    ET = 64

    def after_x(qi):
        q = q_of(qi)

        @pl.loop(0, 2 * H // ET)
        def _(n):
            e = lax.div(n, H // ET)
            prow = jnp.concatenate(
                [pt[2 * q, pl.ds(2 * p + e, 1), :], pt[2 * q + 1, pl.ds(2 * p + e, 1), :]], axis=1
            )
            a = pl.ds(pl.multiple_of(n * ET, ET), ET)
            b = pl.ds(pl.multiple_of(2 * H + n * ET, ET), ET)
            g, u = acc[qi, a, :], acc[qi, b, :]
            s = jax.nn.sigmoid(g)
            active = g * s
            gh[pl.ds(pl.multiple_of(4 * H + n * ET, ET), ET), cols(q)] = (
                active * u * prow
            ).astype(BF16)
            acc[qi, a, :] = u * s * (1.0 + g * (1.0 - s)) * prow
            acc[qi, b, :] = active * prow

    def after_dy(qi):
        q = q_of(qi)

        @pl.loop(0, 2)
        def _(e):
            for kind in range(2):
                lo = kind * 2 * H
                back = acc[qi, pl.ds(pl.multiple_of(4 * H + e * H, H), H), :]
                at = pl.ds(pl.multiple_of(lo + e * H, H), H)
                v = back * acc[qi, at, :]
                gh[at, cols(q)] = v.astype(BF16)
                gT[qi, :, at] = v.T.astype(BF16)

    def forward(qi, s):
        arr, f = lax.div(s, 4), feature_of(lax.rem(s, 4))
        q = q_of(qi)
        got(act.at[arr, f, rows(q * 2 + 1 - c)], gc_r.at[qi, s])
        first = lax.rem(s, 4) == 0

        @pl.loop(0, 4 - 2 * arr)
        def _(n):
            at = pl.ds(pl.multiple_of((4 * arr + n) * H, H), H)
            d = lax.dot_general(
                wv[f, at, :], act[arr, f, cols(q), :], (((1,), (1,)), ((), ())),
                preferred_element_type=F32,
            )

            @pl.when(first)
            def _():
                acc[qi, at, :] = d

            @pl.when(jnp.logical_not(first))
            def _():
                acc[qi, at, :] += d

        @pl.when(s == 3)
        def _():
            after_x(qi)

        @pl.when(s == 7)
        def _():
            after_dy(qi)

    for d in range(1, 8):
        send(pt.at[p], pt.at[p], pt_s.at[d - 1], pt_r.at[d - 1], (z, lax.rem(p + d, 8)))

    @pl.loop(0, 10)
    def _(u):
        @pl.when(u < 8)
        def _():
            col_block(u)

        @pl.when((u >= 1) & (u < 9))
        def _():
            near_blocks(u - 1)

        @pl.when(u >= 2)
        def _():
            far_block(u - 2)

        @pl.when(u == 0)
        def _():
            for r in range(6):
                for f in range(4):
                    w_copy(r, f).wait()
            for d in range(1, 8):
                got(pt.at[lax.rem(p + 8 - d, 8)], pt_r.at[d - 1])

        @pl.loop(0, 4)
        def _(qi):
            s = u - lax.div(qi + 1, 2)

            @pl.when((s >= 0) & (s < 8))
            def _():
                forward(qi, s)

    def quarter_of(k):
        m = 3 - k
        z0, z1 = lax.rem(z, 2), lax.div(z, 2)
        m0, m1 = lax.rem(m, 2), lax.div(m, 2)
        return (z0 + m0 * (1 - 2 * z0)) + 2 * (z1 + m1 * (1 - 2 * z1))

    def parts(k):
        f = quarter_of(k)

        @pl.loop(1, 5)
        def _(i):
            qi = lax.rem(i, 4)
            q = q_of(qi)
            Q[f, cols(q), :] = jnp.dot(
                gT[qi], wv[f, pl.ds(0, 4 * H), :], preferred_element_type=F32
            ).astype(BF16)
            send(
                Q.at[f, rows(q * 2 + 1 - c)], RC.at[k, qi],
                rc_s.at[k, qi], rc_r.at[k, qi], dev_c,
            )

    AT = 32

    def add(dst, size, *terms):
        @pl.loop(0, size // AT)
        def _(n):
            at = pl.ds(pl.multiple_of(n * AT, AT), AT)
            total = dst[at, :].astype(F32)
            for t in terms:
                total = total + t[at, :].astype(F32)
            dst[at, :] = total.astype(BF16)

    def core_sums(k):
        f = quarter_of(k)
        for qi in (1, 2, 3, 0):
            got(RC.at[k, qi], rc_r.at[k, qi])
            add(Q.at[f, rows(block_of(qi))], T, RC.at[k, qi])
            lo = Q.at[f, rows(block_of(qi), 0, half)]
            hi = Q.at[f, rows(block_of(qi), half, half)]
            if qi == 1:
                send(lo, RX.at[0, k], rx_s.at[0, k], rx_r.at[0, k], dev_x)
            elif qi == 2:
                send(hi, RY.at[0, k], ry_s.at[0, k], ry_r.at[0, k], dev_y)
            elif qi == 3:
                send(lo, RX.at[1, k], rx_s.at[1, k], rx_r.at[1, k], dev_x)
                send(hi, RY.at[1, k], ry_s.at[1, k], ry_r.at[1, k], dev_y)

    def turn_sums(k):
        f = quarter_of(k)
        got(RX.at[1, k], rx_r.at[1, k])
        lo = Q.at[f, rows(py, 0, half)]
        add(lo, half, RX.at[1, k])
        send(lo, RY.at[2, k], ry_s.at[2, k], ry_r.at[2, k], dev_y)
        got(RY.at[1, k], ry_r.at[1, k])
        hi = Q.at[f, rows(px, half, half)]
        add(hi, half, RY.at[1, k])
        send(hi, RX.at[2, k], rx_s.at[2, k], rx_r.at[2, k], dev_x)

    def plane_sums(k):
        f = quarter_of(k)
        got(RX.at[0, k], rx_r.at[0, k])
        got(RY.at[2, k], ry_r.at[2, k])
        add(Q.at[f, rows(p, 0, half)], half, RX.at[0, k], RY.at[2, k])
        got(RY.at[0, k], ry_r.at[0, k])
        got(RX.at[2, k], rx_r.at[2, k])
        add(Q.at[f, rows(p, half, half)], half, RY.at[0, k], RX.at[2, k])

        @pl.when(k < 3)
        def _():
            i = 2 - k
            send(Q.at[f, rows(p)], RZ.at[i], rz_s.at[i], rz_r.at[i], (f, p))

    def gw_copy(slot, r, f):
        return pltpu.make_async_copy(
            stage.at[slot],
            gw_ref.at[r, :, pl.ds(pl.multiple_of(f * FC, FC), FC)],
            wg_sem.at[slot],
        )

    def weight_grad(t):
        f, r = lax.div(t, 6), lax.rem(t, 6)
        slot = lax.rem(t, 2)

        @pl.when(t >= 2)
        def _():
            gw_copy(slot, r, f).wait()

        stage[slot] = jnp.dot(
            gh[pl.ds(pl.multiple_of(r * H, H), H), :], act[lax.div(r, 4), f],
            preferred_element_type=F32,
        ).astype(BF16)
        gw_copy(slot, r, f).start()

    @pl.loop(0, 6)
    def _(u):
        @pl.when(u < 4)
        def _():
            parts(u)
            core_sums(u)

        @pl.when((u >= 1) & (u < 5))
        def _():
            turn_sums(u - 1)

        @pl.when(u >= 2)
        def _():
            plane_sums(u - 2)

        @pl.loop(0, 4)
        def _(n):
            weight_grad(u * 4 + n)

    for i in range(3):
        got(RZ.at[i], rz_r.at[i])

    @pl.loop(0, T // AT)
    def _(n):
        at = pl.ds(pl.multiple_of(n * AT, AT), AT)
        total = Q[z, pl.ds(pl.multiple_of(p * T + n * AT, AT), AT), :].astype(F32)
        for i in range(3):
            total = total + RZ[i, at, :].astype(F32)
        outv[at, :] = total.astype(BF16)

    out = pltpu.make_async_copy(outv, gt_ref, out_sem)
    out.start()
    out.wait()
    for t in (22, 23):
        gw_copy(t % 2, t % 6, t // 6).wait()

    for d in range(1, 8):
        got(pt.at[p], pt_s.at[d - 1])

    @pl.loop(0, 8)
    def _(s):
        arr, f = lax.div(s, 4), lax.rem(s, 4)
        ref = act.at[arr, f, rows(p)]
        part = act.at[arr, f, rows(p, 0, half)]

        @pl.when((f <= z) & (z < 3))
        def _():
            got(ref, up_s.at[s])

        @pl.when((f >= z) & (z > 0))
        def _():
            got(ref, dn_s.at[s])

        got(ref, gx_s.at[s])
        got(ref, gy_s.at[s])
        got(part, hx_s.at[s])
        got(part, hy_s.at[s])

        @pl.loop(0, 4)
        def _(qi):
            got(ref, gc_s.at[qi, s])

    @pl.loop(0, 4)
    def _(k):
        @pl.loop(0, 4)
        def _(qi):
            got(RC.at[k, qi], rc_s.at[k, qi])

        for i in range(3):
            got(RX.at[i, k], rx_s.at[i, k])
            got(RY.at[i, k], ry_s.at[i, k])

    for i in range(3):
        got(RZ.at[i], rz_s.at[i])


def dense_body(tokens, grad_out, expert_ids, route_prob, w_gate, w_up, w_down):
    T, FC = tokens.shape
    E, H, D = w_gate.shape
    blocks = lax.axis_size("expert")
    N = blocks * T
    experts = blocks * E
    dma = pltpu.SemaphoreType.DMA
    any_ = pl.BlockSpec(memory_space=pl.ANY)
    vmem = pl.BlockSpec(memory_space=pltpu.VMEM)
    grad_tokens, gw = pl.pallas_call(
        dense_kernel,
        out_shape=(
            jax.ShapeDtypeStruct((T, FC), BF16),
            jax.ShapeDtypeStruct((3 * E, H, D), BF16),
        ),
        in_specs=[any_, any_, vmem, vmem, any_, any_, any_],
        out_specs=(any_, any_),
        scratch_shapes=[
            pltpu.VMEM((2, 4, N, FC), BF16),
            pltpu.VMEM((4, 6 * H, FC), BF16),
            pltpu.VMEM((4, 6 * H, 2 * T), F32),
            pltpu.VMEM((6 * H, N), BF16),
            pltpu.VMEM((4, 2 * T, 4 * H), BF16),
            pltpu.VMEM((4, N, FC), BF16),
            pltpu.VMEM((4, 4, T, FC), BF16),
            pltpu.VMEM((3, 4, T // 2, FC), BF16),
            pltpu.VMEM((3, 4, T // 2, FC), BF16),
            pltpu.VMEM((3, T, FC), BF16),
            pltpu.VMEM((blocks, experts, 128), F32),
            pltpu.VMEM((2, H, FC), BF16),
            pltpu.VMEM((T, FC), BF16),
            dma((6, 4)), dma((2,)), dma((7,)), dma((7,)),
            dma((8,)), dma((8,)), dma((8,)),
            dma((8,)), dma((8,)), dma((8,)), dma((8,)),
            dma((8,)), dma((8,)), dma((8,)), dma((8,)),
            dma((4, 8)), dma((4, 8)), dma((4, 4)), dma((4, 4)),
            dma((3, 4)), dma((3, 4)), dma((3, 4)), dma((3, 4)),
            dma((3,)), dma((3,)), dma((2,)), dma(()),
        ],
        compiler_params=pltpu.CompilerParams(
            collective_id=0, has_side_effects=True, vmem_limit_bytes=60 << 20
        ),
        cost_estimate=pl.CostEstimate(
            flops=2 * N * D * 16 * H, bytes_accessed=12 * E * H * D, transcendentals=N * E * H
        ),
    )(tokens, grad_out, expert_ids, route_prob, w_gate, w_up, w_down)
    return (grad_tokens, gw[:E], gw[E : 2 * E], gw[2 * E :])


def solution(mesh):
    placed = (
        P("expert", "edata"),
        P("expert", "edata"),
        P("expert", None),
        P("expert", None),
        P("expert", "edata", None),
        P("expert", "edata", None),
        P("expert", "edata", None),
    )
    small = mesh.shape["expert"] == 8 and mesh.shape["edata"] == 4
    return jax.shard_map(
        dense_body if small else slots_body,
        mesh=mesh,
        in_specs=placed,
        out_specs=(
            P("expert", "edata"),
            P("expert", "edata", None),
            P("expert", "edata", None),
            P("expert", "edata", None),
        ),
        check_vma=False,
    )
```

```python
import jax
import jax.numpy as jnp
from jax import lax
from jax.experimental import pallas as pl
from jax.experimental.pallas import tpu as pltpu
from jax.sharding import PartitionSpec as P

MESH = pl.DeviceIdType.MESH
BF16 = jnp.bfloat16
F32 = jnp.float32


def ranks(onehot):
    pair_count = onehot.shape[-2]
    row = lax.broadcasted_iota(jnp.int32, (pair_count, pair_count), 0)
    col = lax.broadcasted_iota(jnp.int32, (pair_count, pair_count), 1)
    tri = (col < row).astype(jnp.bfloat16)
    earlier = jnp.einsum(
        "pq,...qe->...pe", tri, onehot.astype(jnp.bfloat16), preferred_element_type=jnp.float32
    )
    return earlier.astype(jnp.int32)


def slots_body(tokens, grad_out, expert_ids, route_prob, w_gate, w_up, w_down):
    token_count, top_count = expert_ids.shape
    local_experts = w_gate.shape[0]
    expert_devices = lax.axis_size("expert")
    me = lax.axis_index("expert")
    experts_all = expert_devices * local_experts
    capacity = token_count * top_count * 5 // (4 * experts_all)
    pair_count = token_count * top_count
    cap_iota = jnp.arange(capacity, dtype=jnp.int32)

    routing = jnp.stack([expert_ids.astype(jnp.float32), route_prob])
    routing = lax.all_gather(routing, "expert", axis=1, tiled=False)
    all_ids, all_prob = routing[0].astype(jnp.int32), routing[1]
    mine = me * local_experts + jnp.arange(local_experts, dtype=jnp.int32)
    named = all_ids.reshape(expert_devices, pair_count)[:, :, None] == mine
    rank = ranks(named)
    hit = named[..., None] & (rank[..., None] == cap_iota)
    hit = hit.reshape(expert_devices, token_count, top_count, local_experts, capacity)
    pick = jnp.sum(hit.astype(jnp.int32), 2).astype(jnp.bfloat16)
    prob_of = jnp.sum(jnp.where(hit, all_prob[:, :, :, None, None], 0.0), (1, 2))

    both = lax.all_gather(jnp.stack([tokens, grad_out]), "edata", axis=2, tiled=True)
    both = lax.all_gather(both, "expert", axis=1, tiled=False)
    all_x, all_dy = both[0], both[1]
    slot_x = jnp.einsum(
        "stxc,std->sxcd", pick, all_x, preferred_element_type=jnp.float32
    ).astype(jnp.bfloat16)
    slot_dy = jnp.einsum("stxc,std->sxcd", pick, all_dy, preferred_element_type=jnp.float32)
    slot_dy = (prob_of[..., None] * slot_dy).astype(jnp.bfloat16)

    gate_value = jnp.einsum("sxcd,xfd->sxcf", slot_x, w_gate, preferred_element_type=jnp.float32)
    up_value = jnp.einsum("sxcd,xfd->sxcf", slot_x, w_up, preferred_element_type=jnp.float32)
    sigma = jax.nn.sigmoid(gate_value)
    active = gate_value * sigma
    hidden = (active * up_value).astype(jnp.bfloat16)
    back = jnp.einsum("sxcd,xfd->sxcf", slot_dy, w_down, preferred_element_type=jnp.float32)
    gate_grad = (back * up_value * sigma * (1.0 + gate_value * (1.0 - sigma))).astype(jnp.bfloat16)
    up_grad = (back * active).astype(jnp.bfloat16)
    grad_gate = jnp.einsum(
        "sxcf,sxcd->xfd", gate_grad, slot_x, preferred_element_type=jnp.float32
    ).astype(jnp.bfloat16)
    grad_up = jnp.einsum(
        "sxcf,sxcd->xfd", up_grad, slot_x, preferred_element_type=jnp.float32
    ).astype(jnp.bfloat16)
    grad_down = jnp.einsum(
        "sxcf,sxcd->xfd", hidden, slot_dy, preferred_element_type=jnp.float32
    ).astype(jnp.bfloat16)
    partial_value = jnp.einsum(
        "sxcf,xfd->sxcd", gate_grad, w_gate, preferred_element_type=jnp.float32
    )
    partial_value = partial_value + jnp.einsum(
        "sxcf,xfd->sxcd", up_grad, w_up, preferred_element_type=jnp.float32
    )
    partial_value = partial_value.astype(jnp.bfloat16)
    returned = lax.all_to_all(
        partial_value.reshape(expert_devices, local_experts * capacity, -1),
        "expert",
        split_axis=0,
        concat_axis=0,
        tiled=True,
    )
    width = returned.shape[-1]

    own = expert_ids.reshape(pair_count, 1) == jnp.arange(experts_all, dtype=jnp.int32)
    slot = jnp.sum(jnp.where(own, ranks(own), 0), 1)
    back_hit = own[:, :, None] & (slot[:, None, None] == cap_iota)
    gather_back = jnp.sum(
        back_hit.reshape(token_count, top_count, experts_all * capacity).astype(jnp.int32), 1
    ).astype(jnp.bfloat16)
    per_token = jnp.einsum(
        "tq,qd->td",
        gather_back,
        returned.reshape(experts_all * capacity, width),
        preferred_element_type=jnp.float32,
    )
    grad_tokens = lax.psum_scatter(per_token, "edata", scatter_dimension=1, tiled=True).astype(
        jnp.bfloat16
    )
    return (grad_tokens, grad_gate, grad_up, grad_down)


def dense_kernel(
    tokens_ref, dy_ref, ids_ref, prob_ref, wg_ref, wu_ref, wd_ref,
    gt_ref, gw_ref,
    act, wv, acc, gh, gT, Q, RC, RX, RY, RZ, pt, stage, outv,
    w_sem, own_sem, pt_s, pt_r, up_s, dn_s, col_r, edge_s, edge_r, tx_s, tx_r, ty_s, ty_r,
    gx_s, gx_r, gy_s, gy_r, hx_s, hx_r, hy_s, hy_r, gc_s, gc_r, rc_s, rc_r, rx_s, rx_r, ry_s, ry_r,
    rz_s, rz_r, wg_sem, out_sem,
):
    T, FC = tokens_ref.shape
    H = wg_ref.shape[1]
    half = T // 2
    z = lax.axis_index("edata")
    p = lax.axis_index("expert")
    c = lax.rem(p, 2)
    x = lax.rem(lax.div(p, 2), 2)
    y = lax.div(p, 4)

    def q_of(qi):
        a, b = qi % 2, qi // 2
        if not isinstance(qi, int):
            a, b = lax.rem(qi, 2), lax.div(qi, 2)
        return (y + b * (1 - 2 * y)) * 2 + (x + a * (1 - 2 * x))

    def block_of(qi):
        return q_of(qi) * 2 + c

    px, py, pd, pc = block_of(1), block_of(2), block_of(3), q_of(0) * 2 + 1 - c
    dev_x, dev_y, dev_c = (z, px), (z, py), (z, pc)

    def rows(block, first=0, size=T):
        return pl.ds(pl.multiple_of(block * T + first, half), size)

    def cols(q):
        return pl.ds(pl.multiple_of(q * 2 * T, 2 * T), 2 * T)

    def feature_of(j):
        hi = lax.div(z, 2)
        zz = hi * (3 - z) + (1 - hi) * z
        near = jnp.where(j == 0, zz, 1 - zz)
        g = jnp.where(j < 2, near, j)
        return hi * (3 - g) + (1 - hi) * g

    def send(src, dst, s_sem, r_sem, dev):
        pltpu.make_async_remote_copy(
            src_ref=src, dst_ref=dst, send_sem=s_sem, recv_sem=r_sem,
            device_id=dev, device_id_type=MESH,
        ).start()

    def got(dst, sem):
        pltpu.make_async_copy(dst, dst, sem).wait()

    wrefs = (wg_ref, wu_ref, wd_ref)

    def w_copy(r, f):
        return pltpu.make_async_copy(
            wrefs[r // 2].at[r % 2, :, pl.ds(f * FC, FC)],
            wv.at[f, pl.ds(r * H, H), :],
            w_sem.at[r, f],
        )

    own_x = pltpu.make_async_copy(tokens_ref, act.at[0, z, rows(p)], own_sem.at[0])
    own_dy = pltpu.make_async_copy(dy_ref, act.at[1, z, rows(p)], own_sem.at[1])
    own_x.start()
    own_dy.start()
    for r in range(6):
        for f in range(4):
            w_copy(r, f).start()

    ids, prob = ids_ref[...], prob_ref[...]
    pt[p] = jnp.concatenate(
        [
            jnp.sum(jnp.where(ids == e, prob, 0.0), axis=0, keepdims=True)
            for e in range(pt.shape[1])
        ],
        axis=0,
    )

    bar = pltpu.get_barrier_semaphore()
    for d in range(1, 8):
        pl.semaphore_signal(bar, inc=1, device_id=(z, lax.rem(p + d, 8)), device_id_type=MESH)
    for d in range(1, 4):
        pl.semaphore_signal(bar, inc=1, device_id=(lax.rem(z + d, 4), p), device_id_type=MESH)
    pl.semaphore_wait(bar, 10)

    for d in range(1, 8):
        send(pt.at[p], pt.at[p], pt_s.at[d - 1], pt_r.at[d - 1], (z, lax.rem(p + d, 8)))

    def chain(ref, i, f):
        i = i * 4 + f

        @pl.when((f <= z) & (z < 3))
        def _():
            send(ref, ref, up_s.at[i], col_r.at[i], (z + 1, p))

        @pl.when((f >= z) & (z > 0))
        def _():
            send(ref, ref, dn_s.at[i], col_r.at[i], (z - 1, p))

    def tok_own(j):
        f = feature_of(j)
        ref = act.at[0, f, rows(p)]
        lo, hi = act.at[0, f, rows(p, 0, half)], act.at[0, f, rows(p, half, half)]

        @pl.when(j == 0)
        def _():
            own_x.wait()

        @pl.when(j > 0)
        def _():
            got(ref, col_r.at[f])

        chain(ref, 0, f)

        @pl.when(j == 0)
        def _():
            send(lo, lo, edge_s.at[0], edge_r.at[0], dev_x)
            send(hi, hi, edge_s.at[1], edge_r.at[1], dev_y)

        send(hi, hi, tx_s.at[0, j], tx_r.at[0, j], dev_x)
        send(lo, lo, ty_s.at[0, j], ty_r.at[0, j], dev_y)
        send(ref, ref, gc_s.at[0, j], gc_r.at[0, j], dev_c)

    def tok_edges(j):
        f = feature_of(j)
        lo, hi = act.at[0, f, rows(px, 0, half)], act.at[0, f, rows(py, half, half)]
        for i, ref in ((0, lo), (1, hi)):
            @pl.when(j == 0)
            def _():
                got(ref, edge_r.at[i])

            @pl.when(j > 0)
            def _():
                got(ref, col_r.at[8 + 4 * i + f])

            chain(ref, 2 + i, f)
            if i == 0:
                send(ref, ref, ty_s.at[1, j], ty_r.at[1, j], dev_y)
            else:
                send(ref, ref, tx_s.at[1, j], tx_r.at[1, j], dev_x)

    def tok_near(j):
        f = feature_of(j)
        got(act.at[0, f, rows(px, half, half)], tx_r.at[0, j])
        rx = act.at[0, f, rows(px)]
        send(rx, rx, gc_s.at[1, j], gc_r.at[1, j], dev_c)
        got(act.at[0, f, rows(py, 0, half)], ty_r.at[0, j])
        ry = act.at[0, f, rows(py)]
        send(ry, ry, gc_s.at[2, j], gc_r.at[2, j], dev_c)

    def tok_far(j):
        f = feature_of(j)
        got(act.at[0, f, rows(pd, half, half)], tx_r.at[1, j])
        got(act.at[0, f, rows(pd, 0, half)], ty_r.at[1, j])
        ref = act.at[0, f, rows(pd)]
        send(ref, ref, gc_s.at[3, j], gc_r.at[3, j], dev_c)

    def cot_own(j):
        f = feature_of(j)
        ref = act.at[1, f, rows(p)]

        @pl.when(j == 0)
        def _():
            own_dy.wait()

        @pl.when(j > 0)
        def _():
            got(ref, col_r.at[4 + f])

        chain(ref, 1, f)
        send(ref, ref, gx_s.at[j], gx_r.at[j], dev_x)
        send(ref, ref, gy_s.at[j], gy_r.at[j], dev_y)
        send(ref, ref, gc_s.at[0, 4 + j], gc_r.at[0, 4 + j], dev_c)

    def cot_near(j):
        f = feature_of(j)
        rx = act.at[1, f, rows(px)]
        got(rx, gx_r.at[j])
        hy = act.at[1, f, rows(px, 0, half)]
        send(hy, hy, hy_s.at[j], hy_r.at[j], dev_y)
        send(rx, rx, gc_s.at[1, 4 + j], gc_r.at[1, 4 + j], dev_c)
        ry = act.at[1, f, rows(py)]
        got(ry, gy_r.at[j])
        hx = act.at[1, f, rows(py, half, half)]
        send(hx, hx, hx_s.at[j], hx_r.at[j], dev_x)
        send(ry, ry, gc_s.at[2, 4 + j], gc_r.at[2, 4 + j], dev_c)

    def cot_far(j):
        f = feature_of(j)
        got(act.at[1, f, rows(pd, 0, half)], hy_r.at[j])
        got(act.at[1, f, rows(pd, half, half)], hx_r.at[j])
        ref = act.at[1, f, rows(pd)]
        send(ref, ref, gc_s.at[3, 4 + j], gc_r.at[3, 4 + j], dev_c)

    ET = 64

    def after_x(qi):
        q = q_of(qi)

        @pl.loop(0, 2 * H // ET)
        def _(n):
            e = lax.div(n, H // ET)
            prow = jnp.concatenate(
                [pt[2 * q, pl.ds(2 * p + e, 1), :], pt[2 * q + 1, pl.ds(2 * p + e, 1), :]], axis=1
            )
            a = pl.ds(pl.multiple_of(n * ET, ET), ET)
            b = pl.ds(pl.multiple_of(2 * H + n * ET, ET), ET)
            g, u = acc[qi, a, :], acc[qi, b, :]
            s = jax.nn.sigmoid(g)
            active = g * s
            gh[pl.ds(pl.multiple_of(4 * H + n * ET, ET), ET), cols(q)] = (
                active * u * prow
            ).astype(BF16)
            acc[qi, a, :] = u * s * (1.0 + g * (1.0 - s)) * prow
            acc[qi, b, :] = active * prow

    def after_dy(qi):
        q = q_of(qi)

        @pl.loop(0, 2)
        def _(e):
            for kind in range(2):
                lo = kind * 2 * H
                back = acc[qi, pl.ds(pl.multiple_of(4 * H + e * H, H), H), :]
                at = pl.ds(pl.multiple_of(lo + e * H, H), H)
                v = back * acc[qi, at, :]
                gh[at, cols(q)] = v.astype(BF16)
                gT[qi, :, at] = v.T.astype(BF16)

    def forward(arr, qi, j):
        f, q = feature_of(j), q_of(qi)
        got(act.at[arr, f, rows(q * 2 + 1 - c)], gc_r.at[qi, arr * 4 + j])

        @pl.loop(4 * arr, 4 + 2 * arr)
        def _(n):
            at = pl.ds(pl.multiple_of(n * H, H), H)
            d = lax.dot_general(
                wv[f, at, :], act[arr, f, cols(q), :], (((1,), (1,)), ((), ())),
                preferred_element_type=F32,
            )

            @pl.when(j == 0)
            def _():
                acc[qi, at, :] = d

            @pl.when(j > 0)
            def _():
                acc[qi, at, :] += d

        @pl.when(j == 3)
        def _():
            if arr:
                after_dy(qi)
            else:
                after_x(qi)

    def both_near(arr, j):
        @pl.loop(1, 3)
        def _(qi):
            forward(arr, qi, j)

    def weights_here():
        for r in range(6):
            for f in range(4):
                w_copy(r, f).wait()
        for d in range(1, 8):
            got(pt.at[lax.rem(p + 8 - d, 8)], pt_r.at[d - 1])

    gather_steps = (
        (2, lambda j: both_near(0, j)),
        (0, tok_own),
        (0, lambda j: pl.when(j == 0)(weights_here)),
        (0, lambda j: forward(0, 0, j)),
        (1, lambda j: forward(1, 0, j)),
        (2, cot_near),
        (3, cot_far),
        (3, lambda j: forward(0, 3, j)),
        (1, tok_edges),
        (1, tok_near),
        (2, tok_far),
        (2, lambda j: both_near(1, j)),
        (3, lambda j: forward(1, 3, j)),
        (0, cot_own),
    )

    def run(steps, u):
        for lag, step in steps:
            @pl.when((u >= lag) & (u < lag + 4))
            def _():
                step(u - lag)

    @pl.loop(0, 7)
    def _(u):
        run(gather_steps, u)

    def quarter_of(k):
        m = 3 - k
        z0, z1 = lax.rem(z, 2), lax.div(z, 2)
        m0, m1 = lax.rem(m, 2), lax.div(m, 2)
        return (z0 + m0 * (1 - 2 * z0)) + 2 * (z1 + m1 * (1 - 2 * z1))

    def part(qi, k):
        f, q = quarter_of(k), q_of(qi)
        Q[f, cols(q), :] = jnp.dot(
            gT[qi], wv[f, pl.ds(0, 4 * H), :], preferred_element_type=F32
        ).astype(BF16)
        send(
            Q.at[f, rows(q * 2 + 1 - c)], RC.at[k, qi],
            rc_s.at[k, qi], rc_r.at[k, qi], dev_c,
        )

    AT = 32

    def add(dst, size, *terms):
        @pl.loop(0, size // AT)
        def _(n):
            at = pl.ds(pl.multiple_of(n * AT, AT), AT)
            total = dst[at, :].astype(F32)
            for t in terms:
                total = total + t[at, :].astype(F32)
            dst[at, :] = total.astype(BF16)

    def core_sum(qi, k):
        f = quarter_of(k)
        got(RC.at[k, qi], rc_r.at[k, qi])
        add(Q.at[f, rows(block_of(qi))], T, RC.at[k, qi])
        lo = Q.at[f, rows(block_of(qi), 0, half)]
        hi = Q.at[f, rows(block_of(qi), half, half)]
        if qi == 1:
            send(lo, RX.at[0, k], rx_s.at[0, k], rx_r.at[0, k], dev_x)
        elif qi == 2:
            send(hi, RY.at[0, k], ry_s.at[0, k], ry_r.at[0, k], dev_y)
        elif qi == 3:
            send(lo, RX.at[1, k], rx_s.at[1, k], rx_r.at[1, k], dev_x)
            send(hi, RY.at[1, k], ry_s.at[1, k], ry_r.at[1, k], dev_y)

    def turn_sums(k):
        f = quarter_of(k)
        got(RX.at[1, k], rx_r.at[1, k])
        lo = Q.at[f, rows(py, 0, half)]
        add(lo, half, RX.at[1, k])
        send(lo, RY.at[2, k], ry_s.at[2, k], ry_r.at[2, k], dev_y)
        got(RY.at[1, k], ry_r.at[1, k])
        hi = Q.at[f, rows(px, half, half)]
        add(hi, half, RY.at[1, k])
        send(hi, RX.at[2, k], rx_s.at[2, k], rx_r.at[2, k], dev_x)

    def plane_sums(k):
        f = quarter_of(k)
        got(RX.at[0, k], rx_r.at[0, k])
        got(RY.at[2, k], ry_r.at[2, k])
        add(Q.at[f, rows(p, 0, half)], half, RX.at[0, k], RY.at[2, k])
        got(RY.at[0, k], ry_r.at[0, k])
        got(RX.at[2, k], rx_r.at[2, k])
        add(Q.at[f, rows(p, half, half)], half, RY.at[0, k], RX.at[2, k])

        @pl.when(k < 3)
        def _():
            i = 2 - k
            send(Q.at[f, rows(p)], RZ.at[i], rz_s.at[i], rz_r.at[i], (f, p))

    def gw_copy(slot, r, f):
        return pltpu.make_async_copy(
            stage.at[slot],
            gw_ref.at[r, :, pl.ds(pl.multiple_of(f * FC, FC), FC)],
            wg_sem.at[slot],
        )

    def weight_grad(t):
        f, r = lax.div(t, 6), lax.rem(t, 6)
        slot = lax.rem(t, 2)

        @pl.when(t >= 2)
        def _():
            gw_copy(slot, r, f).wait()

        stage[slot] = jnp.dot(
            gh[pl.ds(pl.multiple_of(r * H, H), H), :], act[lax.div(r, 4), f],
            preferred_element_type=F32,
        ).astype(BF16)
        gw_copy(slot, r, f).start()

    @pl.loop(0, 5)
    def _(u):
        run(
            (
                (0, lambda k: part(3, k)),
                (1, lambda k: part(0, k)),
                (0, lambda k: part(2, k)),
                (0, lambda k: part(1, k)),
                (0, lambda k: core_sum(3, k)),
            ),
            u,
        )

        @pl.loop(0, 3)
        def _(n):
            weight_grad(u * 5 + n)

        run(
            (
                (1, lambda k: core_sum(0, k)),
                (0, lambda k: core_sum(2, k)),
                (0, lambda k: core_sum(1, k)),
                (1, plane_sums),
            ),
            u,
        )

        @pl.loop(3, 5 - lax.div(u, 4))
        def _(n):
            weight_grad(u * 5 + n)

        run(((0, turn_sums),), u)

    for i in range(3):
        got(RZ.at[i], rz_r.at[i])

    @pl.loop(0, T // AT)
    def _(n):
        at = pl.ds(pl.multiple_of(n * AT, AT), AT)
        total = Q[z, pl.ds(pl.multiple_of(p * T + n * AT, AT), AT), :].astype(F32)
        for i in range(3):
            total = total + RZ[i, at, :].astype(F32)
        outv[at, :] = total.astype(BF16)

    out = pltpu.make_async_copy(outv, gt_ref, out_sem)
    out.start()
    out.wait()
    for t in (22, 23):
        gw_copy(t % 2, t % 6, t // 6).wait()

    for d in range(1, 8):
        got(pt.at[p], pt_s.at[d - 1])

    def sent_along(i, f):
        ref = act.at[0, f, rows(p)] if i < 2 else act.at[0, f, rows(p, 0, half)]

        @pl.when((f <= z) & (z < 3))
        def _():
            got(ref, up_s.at[i * 4 + f])

        @pl.when((f >= z) & (z > 0))
        def _():
            got(ref, dn_s.at[i * 4 + f])

    part_ref = act.at[0, 0, rows(p, 0, half)]
    got(part_ref, edge_s.at[0])
    got(part_ref, edge_s.at[1])

    @pl.loop(0, 4)
    def _(j):
        for i in range(4):
            sent_along(i, j)
        for i in range(2):
            got(part_ref, tx_s.at[i, j])
            got(part_ref, ty_s.at[i, j])
        ref = act.at[0, 0, rows(p)]
        got(ref, gx_s.at[j])
        got(ref, gy_s.at[j])
        got(part_ref, hx_s.at[j])
        got(part_ref, hy_s.at[j])
        for i in range(4):
            got(ref, gc_s.at[i, j])
            got(ref, gc_s.at[i, 4 + j])

    @pl.loop(0, 4)
    def _(k):
        @pl.loop(0, 4)
        def _(qi):
            got(RC.at[k, qi], rc_s.at[k, qi])

        for i in range(3):
            got(RX.at[i, k], rx_s.at[i, k])
            got(RY.at[i, k], ry_s.at[i, k])

    for i in range(3):
        got(RZ.at[i], rz_s.at[i])


def dense_body(tokens, grad_out, expert_ids, route_prob, w_gate, w_up, w_down):
    T, FC = tokens.shape
    E, H, D = w_gate.shape
    blocks = lax.axis_size("expert")
    N = blocks * T
    experts = blocks * E
    dma = pltpu.SemaphoreType.DMA
    any_ = pl.BlockSpec(memory_space=pl.ANY)
    vmem = pl.BlockSpec(memory_space=pltpu.VMEM)
    grad_tokens, gw = pl.pallas_call(
        dense_kernel,
        out_shape=(
            jax.ShapeDtypeStruct((T, FC), BF16),
            jax.ShapeDtypeStruct((3 * E, H, D), BF16),
        ),
        in_specs=[any_, any_, vmem, vmem, any_, any_, any_],
        out_specs=(any_, any_),
        scratch_shapes=[
            pltpu.VMEM((2, 4, N, FC), BF16),
            pltpu.VMEM((4, 6 * H, FC), BF16),
            pltpu.VMEM((4, 6 * H, 2 * T), F32),
            pltpu.VMEM((6 * H, N), BF16),
            pltpu.VMEM((4, 2 * T, 4 * H), BF16),
            pltpu.VMEM((4, N, FC), BF16),
            pltpu.VMEM((4, 4, T, FC), BF16),
            pltpu.VMEM((3, 4, T // 2, FC), BF16),
            pltpu.VMEM((3, 4, T // 2, FC), BF16),
            pltpu.VMEM((3, T, FC), BF16),
            pltpu.VMEM((blocks, experts, 128), F32),
            pltpu.VMEM((2, H, FC), BF16),
            pltpu.VMEM((T, FC), BF16),
            dma((6, 4)), dma((2,)), dma((7,)), dma((7,)),
            dma((16,)), dma((16,)), dma((16,)), dma((2,)), dma((2,)),
            dma((2, 4)), dma((2, 4)), dma((2, 4)), dma((2, 4)),
            dma((4,)), dma((4,)), dma((4,)), dma((4,)),
            dma((4,)), dma((4,)), dma((4,)), dma((4,)),
            dma((4, 8)), dma((4, 8)), dma((4, 4)), dma((4, 4)),
            dma((3, 4)), dma((3, 4)), dma((3, 4)), dma((3, 4)),
            dma((3,)), dma((3,)), dma((2,)), dma(()),
        ],
        compiler_params=pltpu.CompilerParams(
            collective_id=0, has_side_effects=True, vmem_limit_bytes=60 << 20
        ),
        cost_estimate=pl.CostEstimate(
            flops=2 * N * D * 16 * H, bytes_accessed=12 * E * H * D, transcendentals=N * E * H
        ),
    )(tokens, grad_out, expert_ids.T, route_prob.T, w_gate, w_up, w_down)
    return (grad_tokens, gw[:E], gw[E : 2 * E], gw[2 * E :])


def solution(mesh):
    placed = (
        P("expert", "edata"),
        P("expert", "edata"),
        P("expert", None),
        P("expert", None),
        P("expert", "edata", None),
        P("expert", "edata", None),
        P("expert", "edata", None),
    )
    small = mesh.shape["expert"] == 8 and mesh.shape["edata"] == 4
    return jax.shard_map(
        dense_body if small else slots_body,
        mesh=mesh,
        in_specs=placed,
        out_specs=(
            P("expert", "edata"),
            P("expert", "edata", None),
            P("expert", "edata", None),
            P("expert", "edata", None),
        ),
        check_vma=False,
    )
```

```python
import jax
import jax.numpy as jnp
from jax import lax
from jax.experimental import pallas as pl
from jax.experimental.pallas import tpu as pltpu
from jax.sharding import PartitionSpec as P

MESH = pl.DeviceIdType.MESH
BF16 = jnp.bfloat16
F32 = jnp.float32


def ranks(onehot):
    pair_count = onehot.shape[-2]
    row = lax.broadcasted_iota(jnp.int32, (pair_count, pair_count), 0)
    col = lax.broadcasted_iota(jnp.int32, (pair_count, pair_count), 1)
    tri = (col < row).astype(jnp.bfloat16)
    earlier = jnp.einsum(
        "pq,...qe->...pe", tri, onehot.astype(jnp.bfloat16), preferred_element_type=jnp.float32
    )
    return earlier.astype(jnp.int32)


def slots_body(tokens, grad_out, expert_ids, route_prob, w_gate, w_up, w_down):
    token_count, top_count = expert_ids.shape
    local_experts = w_gate.shape[0]
    expert_devices = lax.axis_size("expert")
    me = lax.axis_index("expert")
    experts_all = expert_devices * local_experts
    capacity = token_count * top_count * 5 // (4 * experts_all)
    pair_count = token_count * top_count
    cap_iota = jnp.arange(capacity, dtype=jnp.int32)

    routing = jnp.stack([expert_ids.astype(jnp.float32), route_prob])
    routing = lax.all_gather(routing, "expert", axis=1, tiled=False)
    all_ids, all_prob = routing[0].astype(jnp.int32), routing[1]
    mine = me * local_experts + jnp.arange(local_experts, dtype=jnp.int32)
    named = all_ids.reshape(expert_devices, pair_count)[:, :, None] == mine
    rank = ranks(named)
    hit = named[..., None] & (rank[..., None] == cap_iota)
    hit = hit.reshape(expert_devices, token_count, top_count, local_experts, capacity)
    pick = jnp.sum(hit.astype(jnp.int32), 2).astype(jnp.bfloat16)
    prob_of = jnp.sum(jnp.where(hit, all_prob[:, :, :, None, None], 0.0), (1, 2))

    both = lax.all_gather(jnp.stack([tokens, grad_out]), "edata", axis=2, tiled=True)
    both = lax.all_gather(both, "expert", axis=1, tiled=False)
    all_x, all_dy = both[0], both[1]
    slot_x = jnp.einsum(
        "stxc,std->sxcd", pick, all_x, preferred_element_type=jnp.float32
    ).astype(jnp.bfloat16)
    slot_dy = jnp.einsum("stxc,std->sxcd", pick, all_dy, preferred_element_type=jnp.float32)
    slot_dy = (prob_of[..., None] * slot_dy).astype(jnp.bfloat16)

    gate_value = jnp.einsum("sxcd,xfd->sxcf", slot_x, w_gate, preferred_element_type=jnp.float32)
    up_value = jnp.einsum("sxcd,xfd->sxcf", slot_x, w_up, preferred_element_type=jnp.float32)
    sigma = jax.nn.sigmoid(gate_value)
    active = gate_value * sigma
    hidden = (active * up_value).astype(jnp.bfloat16)
    back = jnp.einsum("sxcd,xfd->sxcf", slot_dy, w_down, preferred_element_type=jnp.float32)
    gate_grad = (back * up_value * sigma * (1.0 + gate_value * (1.0 - sigma))).astype(jnp.bfloat16)
    up_grad = (back * active).astype(jnp.bfloat16)
    grad_gate = jnp.einsum(
        "sxcf,sxcd->xfd", gate_grad, slot_x, preferred_element_type=jnp.float32
    ).astype(jnp.bfloat16)
    grad_up = jnp.einsum(
        "sxcf,sxcd->xfd", up_grad, slot_x, preferred_element_type=jnp.float32
    ).astype(jnp.bfloat16)
    grad_down = jnp.einsum(
        "sxcf,sxcd->xfd", hidden, slot_dy, preferred_element_type=jnp.float32
    ).astype(jnp.bfloat16)
    partial_value = jnp.einsum(
        "sxcf,xfd->sxcd", gate_grad, w_gate, preferred_element_type=jnp.float32
    )
    partial_value = partial_value + jnp.einsum(
        "sxcf,xfd->sxcd", up_grad, w_up, preferred_element_type=jnp.float32
    )
    partial_value = partial_value.astype(jnp.bfloat16)
    returned = lax.all_to_all(
        partial_value.reshape(expert_devices, local_experts * capacity, -1),
        "expert",
        split_axis=0,
        concat_axis=0,
        tiled=True,
    )
    width = returned.shape[-1]

    own = expert_ids.reshape(pair_count, 1) == jnp.arange(experts_all, dtype=jnp.int32)
    slot = jnp.sum(jnp.where(own, ranks(own), 0), 1)
    back_hit = own[:, :, None] & (slot[:, None, None] == cap_iota)
    gather_back = jnp.sum(
        back_hit.reshape(token_count, top_count, experts_all * capacity).astype(jnp.int32), 1
    ).astype(jnp.bfloat16)
    per_token = jnp.einsum(
        "tq,qd->td",
        gather_back,
        returned.reshape(experts_all * capacity, width),
        preferred_element_type=jnp.float32,
    )
    grad_tokens = lax.psum_scatter(per_token, "edata", scatter_dimension=1, tiled=True).astype(
        jnp.bfloat16
    )
    return (grad_tokens, grad_gate, grad_up, grad_down)


def dense_kernel(
    tokens_ref, dy_ref, ids_ref, prob_ref, wg_ref, wu_ref, wd_ref,
    gt_ref, gw_ref,
    act, wv, gh, gT, RC, RX, RY, RZ, pt,
    w_sem, own_sem, pt_s, pt_r, up_s, dn_s, col_r, edge_s, edge_r, tx_s, tx_r, ty_s, ty_r,
    gx_s, gx_r, gy_s, gy_r, hx_s, hx_r, hy_s, hy_r, gc_s, gc_r, rc_s, rc_r, rx_s, rx_r, ry_s, ry_r,
    rz_s, rz_r,
):
    T, FC = tokens_ref.shape
    H = wg_ref.shape[1]
    half = T // 2
    z = lax.axis_index("edata")
    p = lax.axis_index("expert")
    c = lax.rem(p, 2)
    x = lax.rem(lax.div(p, 2), 2)
    y = lax.div(p, 4)

    def q_of(qi):
        a, b = qi % 2, qi // 2
        if not isinstance(qi, int):
            a, b = lax.rem(qi, 2), lax.div(qi, 2)
        return (y + b * (1 - 2 * y)) * 2 + (x + a * (1 - 2 * x))

    def block_of(qi):
        return q_of(qi) * 2 + c

    px, py, pd, pc = block_of(1), block_of(2), block_of(3), q_of(0) * 2 + 1 - c
    dev_x, dev_y, dev_c = (z, px), (z, py), (z, pc)

    def rows(block, first=0, size=T):
        return pl.ds(pl.multiple_of(block * T + first, half), size)

    def cols(q):
        return pl.ds(pl.multiple_of(q * 2 * T, 2 * T), 2 * T)

    def feature_of(j):
        hi = lax.div(z, 2)
        zz = hi * (3 - z) + (1 - hi) * z
        near = jnp.where(j == 0, zz, 1 - zz)
        g = jnp.where(j < 2, near, j)
        return hi * (3 - g) + (1 - hi) * g

    def send(src, dst, s_sem, r_sem, dev):
        pltpu.make_async_remote_copy(
            src_ref=src, dst_ref=dst, send_sem=s_sem, recv_sem=r_sem,
            device_id=dev, device_id_type=MESH,
        ).start()

    def got(dst, sem):
        pltpu.make_async_copy(dst, dst, sem).wait()

    wrefs = (wg_ref, wu_ref, wd_ref)

    def w_copy(r, f):
        return pltpu.make_async_copy(
            wrefs[r // 2].at[r % 2, :, pl.ds(f * FC, FC)],
            wv.at[f, pl.ds(r * H, H), :],
            w_sem.at[r, f],
        )

    own_x = pltpu.make_async_copy(tokens_ref, act.at[0, z, rows(p)], own_sem.at[0])
    own_dy = pltpu.make_async_copy(dy_ref, act.at[1, z, rows(p)], own_sem.at[1])
    own_x.start()
    own_dy.start()
    for r in range(6):
        for f in range(4):
            w_copy(r, f).start()

    ids, prob = ids_ref[...], prob_ref[...]
    pt[p] = jnp.concatenate(
        [
            jnp.sum(jnp.where(ids == e, prob, 0.0), axis=0, keepdims=True)
            for e in range(pt.shape[1])
        ],
        axis=0,
    )

    bar = pltpu.get_barrier_semaphore()
    for d in range(1, 8):
        pl.semaphore_signal(bar, inc=1, device_id=(z, lax.rem(p + d, 8)), device_id_type=MESH)
    for d in range(1, 4):
        pl.semaphore_signal(bar, inc=1, device_id=(lax.rem(z + d, 4), p), device_id_type=MESH)
    pl.semaphore_wait(bar, 10)

    for d in range(1, 8):
        send(pt.at[p], pt.at[p], pt_s.at[d - 1], pt_r.at[d - 1], (z, lax.rem(p + d, 8)))

    def chain(ref, i, f):
        i = i * 4 + f

        @pl.when((f <= z) & (z < 3))
        def _():
            send(ref, ref, up_s.at[i], col_r.at[i], (z + 1, p))

        @pl.when((f >= z) & (z > 0))
        def _():
            send(ref, ref, dn_s.at[i], col_r.at[i], (z - 1, p))

    def tok_own(j):
        f = feature_of(j)
        ref = act.at[0, f, rows(p)]
        lo, hi = act.at[0, f, rows(p, 0, half)], act.at[0, f, rows(p, half, half)]

        @pl.when(j == 0)
        def _():
            own_x.wait()

        @pl.when(j > 0)
        def _():
            got(ref, col_r.at[f])

        chain(ref, 0, f)

        @pl.when(j == 0)
        def _():
            send(lo, lo, edge_s.at[0], edge_r.at[0], dev_x)
            send(hi, hi, edge_s.at[1], edge_r.at[1], dev_y)

    def tok_spread(j):
        f = feature_of(j)
        ref = act.at[0, f, rows(p)]
        lo, hi = act.at[0, f, rows(p, 0, half)], act.at[0, f, rows(p, half, half)]
        send(hi, hi, tx_s.at[0, j], tx_r.at[0, j], dev_x)
        send(lo, lo, ty_s.at[0, j], ty_r.at[0, j], dev_y)
        send(ref, ref, gc_s.at[0, j], gc_r.at[0, j], dev_c)

    def tok_edge(i, j):
        f = feature_of(j)
        block, first = (py, half) if i else (px, 0)
        ref = act.at[0, f, rows(block, first, half)]

        @pl.when(j == 0)
        def _():
            got(ref, edge_r.at[i])

        @pl.when(j > 0)
        def _():
            got(ref, col_r.at[8 + 4 * i + f])

        chain(ref, 2 + i, f)
        if i:
            send(ref, ref, tx_s.at[1, j], tx_r.at[1, j], dev_x)
        else:
            send(ref, ref, ty_s.at[1, j], ty_r.at[1, j], dev_y)

    def tok_near(i, j):
        f = feature_of(j)
        block, first, sem = (py, 0, ty_r) if i else (px, half, tx_r)
        got(act.at[0, f, rows(block, first, half)], sem.at[0, j])
        ref = act.at[0, f, rows(block)]
        send(ref, ref, gc_s.at[1 + i, j], gc_r.at[1 + i, j], dev_c)

    def tok_far(j):
        f = feature_of(j)
        got(act.at[0, f, rows(pd, half, half)], tx_r.at[1, j])
        got(act.at[0, f, rows(pd, 0, half)], ty_r.at[1, j])
        ref = act.at[0, f, rows(pd)]
        send(ref, ref, gc_s.at[3, j], gc_r.at[3, j], dev_c)

    def cot_own(j):
        f = feature_of(j)
        ref = act.at[1, f, rows(p)]

        @pl.when(j == 0)
        def _():
            own_dy.wait()

        @pl.when(j > 0)
        def _():
            got(ref, col_r.at[4 + f])

        chain(ref, 1, f)

    def cot_spread(j):
        ref = act.at[1, feature_of(j), rows(p)]
        send(ref, ref, gx_s.at[j], gx_r.at[j], dev_x)
        send(ref, ref, gy_s.at[j], gy_r.at[j], dev_y)
        send(ref, ref, gc_s.at[0, 4 + j], gc_r.at[0, 4 + j], dev_c)

    def cot_near(i, j):
        f = feature_of(j)
        block, sem = (py, gy_r) if i else (px, gx_r)
        ref = act.at[1, f, rows(block)]
        got(ref, sem.at[j])
        if i:
            on = act.at[1, f, rows(block, half, half)]
            send(on, on, hx_s.at[j], hx_r.at[j], dev_x)
        else:
            on = act.at[1, f, rows(block, 0, half)]
            send(on, on, hy_s.at[j], hy_r.at[j], dev_y)
        send(ref, ref, gc_s.at[1 + i, 4 + j], gc_r.at[1 + i, 4 + j], dev_c)

    def cot_far(j):
        f = feature_of(j)
        got(act.at[1, f, rows(pd, 0, half)], hy_r.at[j])
        got(act.at[1, f, rows(pd, half, half)], hx_r.at[j])
        ref = act.at[1, f, rows(pd)]
        send(ref, ref, gc_s.at[3, 4 + j], gc_r.at[3, 4 + j], dev_c)

    ET = 64

    def after_x(qi):
        q = q_of(qi)

        @pl.loop(0, 2 * H // ET)
        def _(n):
            e = lax.div(n, H // ET)
            prow = jnp.concatenate(
                [pt[2 * q, pl.ds(2 * p + e, 1), :], pt[2 * q + 1, pl.ds(2 * p + e, 1), :]], axis=1
            )
            a = pl.ds(pl.multiple_of(n * ET, ET), ET)
            b = pl.ds(pl.multiple_of(2 * H + n * ET, ET), ET)
            g, u = acc[qi, a, :], acc[qi, b, :]
            s = jax.nn.sigmoid(g)
            active = g * s
            gh[pl.ds(pl.multiple_of(4 * H + n * ET, ET), ET), cols(q)] = (
                active * u * prow
            ).astype(BF16)
            acc[qi, a, :] = u * s * (1.0 + g * (1.0 - s)) * prow
            acc[qi, b, :] = active * prow

    def after_dy(qi):
        q = q_of(qi)

        @pl.loop(0, 2)
        def _(e):
            for kind in range(2):
                lo = kind * 2 * H
                back = acc[qi, pl.ds(pl.multiple_of(4 * H + e * H, H), H), :]
                at = pl.ds(pl.multiple_of(lo + e * H, H), H)
                v = back * acc[qi, at, :]
                gh[at, cols(q)] = v.astype(BF16)
                gT[qi, :, at] = v.T.astype(BF16)

    def forward(arr, qi, j):
        f, q = feature_of(j), q_of(qi)
        got(act.at[arr, f, rows(q * 2 + 1 - c)], gc_r.at[qi, arr * 4 + j])

        @pl.loop(2 * arr, 2 + arr)
        def _(n):
            at = pl.ds(pl.multiple_of(n * 2 * H, 2 * H), 2 * H)
            d = lax.dot_general(
                wv[f, at, :], act[arr, f, cols(q), :], (((1,), (1,)), ((), ())),
                preferred_element_type=F32,
            )

            @pl.when(j == 0)
            def _():
                acc[qi, at, :] = d

            @pl.when(j > 0)
            def _():
                acc[qi, at, :] += d

        @pl.when(j == 3)
        def _():
            if arr:
                after_dy(qi)
            else:
                after_x(qi)

    def both_near(arr, j):
        @pl.loop(1, 3)
        def _(qi):
            forward(arr, qi, j)

    def weights_here():
        for r in range(6):
            for f in range(4):
                w_copy(r, f).wait()
        for d in range(1, 8):
            got(pt.at[lax.rem(p + 8 - d, 8)], pt_r.at[d - 1])

    gather_steps = (
        (2, lambda j: both_near(0, j)),
        (0, tok_own),
        (0, tok_spread),
        (0, lambda j: pl.when(j == 0)(weights_here)),
        (0, lambda j: forward(0, 0, j)),
        (1, lambda j: forward(1, 0, j)),
        (2, lambda j: cot_near(0, j)),
        (4, lambda j: forward(1, 3, j)),
        (2, lambda j: cot_near(1, j)),
        (1, lambda j: tok_edge(0, j)),
        (3, cot_far),
        (2, tok_far),
        (1, lambda j: tok_near(0, j)),
        (3, lambda j: forward(0, 3, j)),
        (2, lambda j: both_near(1, j)),
        (1, lambda j: tok_edge(1, j)),
        (1, lambda j: tok_near(1, j)),
        (0, cot_own),
        (0, cot_spread),
    )

    def run(steps, u):
        for lag, step in steps:
            @pl.when((u >= lag) & (u < lag + 4))
            def _():
                step(u - lag)

    def gather(buf):
        nonlocal acc
        acc = buf

        @pl.loop(0, 8)
        def _(u):
            run(gather_steps, u)

    acc = Q = None
    pl.run_scoped(gather, pltpu.VMEM((4, 6 * H, 2 * T), F32))

    def quarter_of(k):
        m = 3 - k
        z0, z1 = lax.rem(z, 2), lax.div(z, 2)
        m0, m1 = lax.rem(m, 2), lax.div(m, 2)
        return (z0 + m0 * (1 - 2 * z0)) + 2 * (z1 + m1 * (1 - 2 * z1))

    def part(qi, k):
        f, q = quarter_of(k), q_of(qi)
        Q[f, cols(q), :] = jnp.dot(
            gT[qi], wv[f, pl.ds(0, 4 * H), :], preferred_element_type=F32
        ).astype(BF16)
        send(
            Q.at[f, rows(q * 2 + 1 - c)], RC.at[k, qi],
            rc_s.at[k, qi], rc_r.at[k, qi], dev_c,
        )

    AT = 32

    def add(dst, size, *terms):
        @pl.loop(0, size // AT)
        def _(n):
            at = pl.ds(pl.multiple_of(n * AT, AT), AT)
            total = dst[at, :].astype(F32)
            for t in terms:
                total = total + t[at, :].astype(F32)
            dst[at, :] = total.astype(BF16)

    def core_sum(qi, k):
        f = quarter_of(k)
        got(RC.at[k, qi], rc_r.at[k, qi])
        add(Q.at[f, rows(block_of(qi))], T, RC.at[k, qi])
        lo = Q.at[f, rows(block_of(qi), 0, half)]
        hi = Q.at[f, rows(block_of(qi), half, half)]
        if qi == 1:
            send(lo, RX.at[0, k], rx_s.at[0, k], rx_r.at[0, k], dev_x)
        elif qi == 2:
            send(hi, RY.at[0, k], ry_s.at[0, k], ry_r.at[0, k], dev_y)
        elif qi == 3:
            send(lo, RX.at[1, k], rx_s.at[1, k], rx_r.at[1, k], dev_x)
            send(hi, RY.at[1, k], ry_s.at[1, k], ry_r.at[1, k], dev_y)

    def turn_sums(k):
        f = quarter_of(k)
        got(RX.at[1, k], rx_r.at[1, k])
        lo = Q.at[f, rows(py, 0, half)]
        add(lo, half, RX.at[1, k])
        send(lo, RY.at[2, k], ry_s.at[2, k], ry_r.at[2, k], dev_y)
        got(RY.at[1, k], ry_r.at[1, k])
        hi = Q.at[f, rows(px, half, half)]
        add(hi, half, RY.at[1, k])
        send(hi, RX.at[2, k], rx_s.at[2, k], rx_r.at[2, k], dev_x)

    def plane_sums(k):
        f = quarter_of(k)
        got(RX.at[0, k], rx_r.at[0, k])
        got(RY.at[2, k], ry_r.at[2, k])
        add(Q.at[f, rows(p, 0, half)], half, RX.at[0, k], RY.at[2, k])
        got(RY.at[0, k], ry_r.at[0, k])
        got(RX.at[2, k], rx_r.at[2, k])
        add(Q.at[f, rows(p, half, half)], half, RY.at[0, k], RX.at[2, k])

        @pl.when(k < 3)
        def _():
            i = 2 - k
            send(Q.at[f, rows(p)], RZ.at[i], rz_s.at[i], rz_r.at[i], (f, p))

    def weight_grad(t):
        f, r = lax.div(t, 6), lax.rem(t, 6)
        gw_ref[r, :, pl.ds(pl.multiple_of(f * FC, FC), FC)] = jnp.dot(
            gh[pl.ds(pl.multiple_of(r * H, H), H), :], act[lax.div(r, 4), f],
            preferred_element_type=F32,
        ).astype(BF16)

    return_steps = (
        (1, turn_sums),
        (0, lambda k: part(3, k)),
        (0, lambda k: part(2, k)),
        (0, lambda k: part(1, k)),
        (0, lambda k: core_sum(3, k)),
        (1, lambda k: part(0, k)),
    )
    more_return_steps = (
        (0, lambda k: core_sum(2, k)),
        (0, lambda k: core_sum(1, k)),
        (1, lambda k: core_sum(0, k)),
        (1, plane_sums),
    )

    def all_sent():
        for d in range(1, 8):
            got(pt.at[p], pt_s.at[d - 1])

        def sent_along(i, f):
            ref = act.at[0, f, rows(p)] if i < 2 else act.at[0, f, rows(p, 0, half)]

            @pl.when((f <= z) & (z < 3))
            def _():
                got(ref, up_s.at[i * 4 + f])

            @pl.when((f >= z) & (z > 0))
            def _():
                got(ref, dn_s.at[i * 4 + f])

        part_ref = act.at[0, 0, rows(p, 0, half)]
        got(part_ref, edge_s.at[0])
        got(part_ref, edge_s.at[1])

        @pl.loop(0, 4)
        def _(j):
            for i in range(4):
                sent_along(i, j)
            for i in range(2):
                got(part_ref, tx_s.at[i, j])
                got(part_ref, ty_s.at[i, j])
            ref = act.at[0, 0, rows(p)]
            got(ref, gx_s.at[j])
            got(ref, gy_s.at[j])
            got(part_ref, hx_s.at[j])
            got(part_ref, hy_s.at[j])
            for i in range(4):
                got(ref, gc_s.at[i, j])
                got(ref, gc_s.at[i, 4 + j])

        @pl.loop(0, 4)
        def _(k):
            @pl.loop(0, 4)
            def _(qi):
                got(RC.at[k, qi], rc_s.at[k, qi])

            for i in range(3):
                got(RX.at[i, k], rx_s.at[i, k])
                got(RY.at[i, k], ry_s.at[i, k])

    def give_back(buf):
        nonlocal Q
        Q = buf

        @pl.loop(0, 5)
        def _(u):
            run(return_steps, u)

            @pl.loop(0, 3)
            def _(n):
                weight_grad(u * 5 + n)

            run(more_return_steps, u)

            @pl.loop(3, 5 - lax.div(u, 4))
            def _(n):
                weight_grad(u * 5 + n)

        all_sent()
        for i in range(3):
            got(RZ.at[i], rz_r.at[i])

        @pl.loop(0, T // AT)
        def _(n):
            at = pl.ds(pl.multiple_of(n * AT, AT), AT)
            total = Q[z, pl.ds(pl.multiple_of(p * T + n * AT, AT), AT), :].astype(F32)
            for i in range(3):
                total = total + RZ[i, at, :].astype(F32)
            gt_ref[at, :] = total.astype(BF16)

        for i in range(3):
            got(RZ.at[i], rz_s.at[i])

    pl.run_scoped(give_back, pltpu.VMEM((4, act.shape[2], FC), BF16))


def dense_body(tokens, grad_out, expert_ids, route_prob, w_gate, w_up, w_down):
    T, FC = tokens.shape
    E, H, D = w_gate.shape
    blocks = lax.axis_size("expert")
    N = blocks * T
    experts = blocks * E
    dma = pltpu.SemaphoreType.DMA
    any_ = pl.BlockSpec(memory_space=pl.ANY)
    vmem = pl.BlockSpec(memory_space=pltpu.VMEM)
    grad_tokens, gw = pl.pallas_call(
        dense_kernel,
        out_shape=(pltpu.VMEM((T, FC), BF16), pltpu.VMEM((3 * E, H, D), BF16)),
        in_specs=[any_, any_, vmem, vmem, any_, any_, any_],
        out_specs=(vmem, vmem),
        scratch_shapes=[
            pltpu.VMEM((2, 4, N, FC), BF16),
            pltpu.VMEM((4, 6 * H, FC), BF16),
            pltpu.VMEM((6 * H, N), BF16),
            pltpu.VMEM((4, 2 * T, 4 * H), BF16),
            pltpu.VMEM((4, 4, T, FC), BF16),
            pltpu.VMEM((3, 4, T // 2, FC), BF16),
            pltpu.VMEM((3, 4, T // 2, FC), BF16),
            pltpu.VMEM((3, T, FC), BF16),
            pltpu.VMEM((blocks, experts, 128), F32),
            dma((6, 4)), dma((2,)), dma((7,)), dma((7,)),
            dma((16,)), dma((16,)), dma((16,)), dma((2,)), dma((2,)),
            dma((2, 4)), dma((2, 4)), dma((2, 4)), dma((2, 4)),
            dma((4,)), dma((4,)), dma((4,)), dma((4,)),
            dma((4,)), dma((4,)), dma((4,)), dma((4,)),
            dma((4, 8)), dma((4, 8)), dma((4, 4)), dma((4, 4)),
            dma((3, 4)), dma((3, 4)), dma((3, 4)), dma((3, 4)),
            dma((3,)), dma((3,)),
        ],
        compiler_params=pltpu.CompilerParams(
            collective_id=0, has_side_effects=True, vmem_limit_bytes=51 << 20
        ),
        cost_estimate=pl.CostEstimate(
            flops=2 * N * D * 16 * H, bytes_accessed=12 * E * H * D, transcendentals=N * E * H
        ),
    )(tokens, grad_out, expert_ids.T, route_prob.T, w_gate, w_up, w_down)
    return (grad_tokens, gw[:E], gw[E : 2 * E], gw[2 * E :])


def solution(mesh):
    placed = (
        P("expert", "edata"),
        P("expert", "edata"),
        P("expert", None),
        P("expert", None),
        P("expert", "edata", None),
        P("expert", "edata", None),
        P("expert", "edata", None),
    )
    small = mesh.shape["expert"] == 8 and mesh.shape["edata"] == 4
    return jax.shard_map(
        dense_body if small else slots_body,
        mesh=mesh,
        in_specs=placed,
        out_specs=(
            P("expert", "edata"),
            P("expert", "edata", None),
            P("expert", "edata", None),
            P("expert", "edata", None),
        ),
        check_vma=False,
    )
```

```python
import jax
import jax.numpy as jnp
from jax import lax
from jax.experimental import pallas as pl
from jax.experimental.pallas import tpu as pltpu
from jax.sharding import PartitionSpec as P

MESH = pl.DeviceIdType.MESH
BF16 = jnp.bfloat16
F32 = jnp.float32


def ranks(onehot):
    pair_count = onehot.shape[-2]
    row = lax.broadcasted_iota(jnp.int32, (pair_count, pair_count), 0)
    col = lax.broadcasted_iota(jnp.int32, (pair_count, pair_count), 1)
    tri = (col < row).astype(jnp.bfloat16)
    earlier = jnp.einsum(
        "pq,...qe->...pe", tri, onehot.astype(jnp.bfloat16), preferred_element_type=jnp.float32
    )
    return earlier.astype(jnp.int32)


def slots_body(tokens, grad_out, expert_ids, route_prob, w_gate, w_up, w_down):
    token_count, top_count = expert_ids.shape
    local_experts = w_gate.shape[0]
    expert_devices = lax.axis_size("expert")
    me = lax.axis_index("expert")
    experts_all = expert_devices * local_experts
    capacity = token_count * top_count * 5 // (4 * experts_all)
    pair_count = token_count * top_count
    cap_iota = jnp.arange(capacity, dtype=jnp.int32)

    routing = jnp.stack([expert_ids.astype(jnp.float32), route_prob])
    routing = lax.all_gather(routing, "expert", axis=1, tiled=False)
    all_ids, all_prob = routing[0].astype(jnp.int32), routing[1]
    mine = me * local_experts + jnp.arange(local_experts, dtype=jnp.int32)
    named = all_ids.reshape(expert_devices, pair_count)[:, :, None] == mine
    rank = ranks(named)
    hit = named[..., None] & (rank[..., None] == cap_iota)
    hit = hit.reshape(expert_devices, token_count, top_count, local_experts, capacity)
    pick = jnp.sum(hit.astype(jnp.int32), 2).astype(jnp.bfloat16)
    prob_of = jnp.sum(jnp.where(hit, all_prob[:, :, :, None, None], 0.0), (1, 2))

    both = lax.all_gather(jnp.stack([tokens, grad_out]), "edata", axis=2, tiled=True)
    both = lax.all_gather(both, "expert", axis=1, tiled=False)
    all_x, all_dy = both[0], both[1]
    slot_x = jnp.einsum(
        "stxc,std->sxcd", pick, all_x, preferred_element_type=jnp.float32
    ).astype(jnp.bfloat16)
    slot_dy = jnp.einsum("stxc,std->sxcd", pick, all_dy, preferred_element_type=jnp.float32)
    slot_dy = (prob_of[..., None] * slot_dy).astype(jnp.bfloat16)

    gate_value = jnp.einsum("sxcd,xfd->sxcf", slot_x, w_gate, preferred_element_type=jnp.float32)
    up_value = jnp.einsum("sxcd,xfd->sxcf", slot_x, w_up, preferred_element_type=jnp.float32)
    sigma = jax.nn.sigmoid(gate_value)
    active = gate_value * sigma
    hidden = (active * up_value).astype(jnp.bfloat16)
    back = jnp.einsum("sxcd,xfd->sxcf", slot_dy, w_down, preferred_element_type=jnp.float32)
    gate_grad = (back * up_value * sigma * (1.0 + gate_value * (1.0 - sigma))).astype(jnp.bfloat16)
    up_grad = (back * active).astype(jnp.bfloat16)
    grad_gate = jnp.einsum(
        "sxcf,sxcd->xfd", gate_grad, slot_x, preferred_element_type=jnp.float32
    ).astype(jnp.bfloat16)
    grad_up = jnp.einsum(
        "sxcf,sxcd->xfd", up_grad, slot_x, preferred_element_type=jnp.float32
    ).astype(jnp.bfloat16)
    grad_down = jnp.einsum(
        "sxcf,sxcd->xfd", hidden, slot_dy, preferred_element_type=jnp.float32
    ).astype(jnp.bfloat16)
    partial_value = jnp.einsum(
        "sxcf,xfd->sxcd", gate_grad, w_gate, preferred_element_type=jnp.float32
    )
    partial_value = partial_value + jnp.einsum(
        "sxcf,xfd->sxcd", up_grad, w_up, preferred_element_type=jnp.float32
    )
    partial_value = partial_value.astype(jnp.bfloat16)
    returned = lax.all_to_all(
        partial_value.reshape(expert_devices, local_experts * capacity, -1),
        "expert",
        split_axis=0,
        concat_axis=0,
        tiled=True,
    )
    width = returned.shape[-1]

    own = expert_ids.reshape(pair_count, 1) == jnp.arange(experts_all, dtype=jnp.int32)
    slot = jnp.sum(jnp.where(own, ranks(own), 0), 1)
    back_hit = own[:, :, None] & (slot[:, None, None] == cap_iota)
    gather_back = jnp.sum(
        back_hit.reshape(token_count, top_count, experts_all * capacity).astype(jnp.int32), 1
    ).astype(jnp.bfloat16)
    per_token = jnp.einsum(
        "tq,qd->td",
        gather_back,
        returned.reshape(experts_all * capacity, width),
        preferred_element_type=jnp.float32,
    )
    grad_tokens = lax.psum_scatter(per_token, "edata", scatter_dimension=1, tiled=True).astype(
        jnp.bfloat16
    )
    return (grad_tokens, grad_gate, grad_up, grad_down)


def dense_kernel(
    tokens_ref, dy_ref, ids_ref, prob_ref, wg_ref, wu_ref, wd_ref,
    gt_ref, gw_ref,
    act, wv, gh, gT, RC, RX, RY, RZ, pt,
    w_sem, own_sem, pt_s, pt_r, up_s, dn_s, col_r, edge_s, edge_r, tx_s, tx_r, ty_s, ty_r,
    gx_s, gx_r, gy_s, gy_r, hx_s, hx_r, hy_s, hy_r, gc_s, gc_r, rc_s, rc_r, rx_s, rx_r, ry_s, ry_r,
    rz_s, rz_r,
):
    T, FC = tokens_ref.shape
    H = wg_ref.shape[1]
    half = T // 2
    z = lax.axis_index("edata")
    p = lax.axis_index("expert")
    c = lax.rem(p, 2)
    x = lax.rem(lax.div(p, 2), 2)
    y = lax.div(p, 4)

    def q_of(qi):
        a, b = qi % 2, qi // 2
        if not isinstance(qi, int):
            a, b = lax.rem(qi, 2), lax.div(qi, 2)
        return (y + b * (1 - 2 * y)) * 2 + (x + a * (1 - 2 * x))

    def block_of(qi):
        return q_of(qi) * 2 + c

    px, py, pd, pc = block_of(1), block_of(2), block_of(3), q_of(0) * 2 + 1 - c
    dev_x, dev_y, dev_c = (z, px), (z, py), (z, pc)

    def rows(block, first=0, size=T):
        return pl.ds(pl.multiple_of(block * T + first, half), size)

    def cols(q):
        return pl.ds(pl.multiple_of(q * 2 * T, 2 * T), 2 * T)

    def feature_of(j):
        hi = lax.div(z, 2)
        zz = hi * (3 - z) + (1 - hi) * z
        near = jnp.where(j == 0, zz, 1 - zz)
        g = jnp.where(j < 2, near, j)
        return hi * (3 - g) + (1 - hi) * g

    def send(src, dst, s_sem, r_sem, dev):
        pltpu.make_async_remote_copy(
            src_ref=src, dst_ref=dst, send_sem=s_sem, recv_sem=r_sem,
            device_id=dev, device_id_type=MESH,
        ).start()

    def got(dst, sem):
        pltpu.make_async_copy(dst, dst, sem).wait()

    bar = pltpu.get_barrier_semaphore()
    for d in range(1, 8):
        pl.semaphore_signal(bar, inc=1, device_id=(z, lax.rem(p + d, 8)), device_id_type=MESH)
    for d in range(1, 4):
        pl.semaphore_signal(bar, inc=1, device_id=(lax.rem(z + d, 4), p), device_id_type=MESH)
    own_x = pltpu.make_async_copy(tokens_ref, act.at[0, z, rows(p)], own_sem.at[0])
    own_dy = pltpu.make_async_copy(dy_ref, act.at[1, z, rows(p)], own_sem.at[1])
    own_x.start()
    own_dy.start()
    wrefs = (wg_ref, wu_ref, wd_ref)

    def w_copy(r, j):
        f = feature_of(j)
        return pltpu.make_async_copy(
            wrefs[r // 2].at[r % 2, :, pl.ds(pl.multiple_of(f * FC, FC), FC)],
            wv.at[f, pl.ds(r * H, H), :],
            w_sem.at[r, j],
        )

    def weights_and_routing():
        for j in range(4):
            for r in range(6):
                w_copy(r, j).start()
        ids, prob = ids_ref[...], prob_ref[...]
        pt[p] = jnp.concatenate(
            [
                jnp.sum(jnp.where(ids == e, prob, 0.0), axis=0, keepdims=True)
                for e in range(pt.shape[1])
            ],
            axis=0,
        )
        for d in range(1, 8):
            send(pt.at[p], pt.at[p], pt_s.at[d - 1], pt_r.at[d - 1], (z, lax.rem(p + d, 8)))

    pl.semaphore_wait(bar, 10)

    def chain(ref, i, f):
        i = i * 4 + f

        @pl.when((f <= z) & (z < 3))
        def _():
            send(ref, ref, up_s.at[i], col_r.at[i], (z + 1, p))

        @pl.when((f >= z) & (z > 0))
        def _():
            send(ref, ref, dn_s.at[i], col_r.at[i], (z - 1, p))

    def tok_own(j):
        f = feature_of(j)
        ref = act.at[0, f, rows(p)]
        lo, hi = act.at[0, f, rows(p, 0, half)], act.at[0, f, rows(p, half, half)]

        @pl.when(j == 0)
        def _():
            own_x.wait()

        @pl.when(j > 0)
        def _():
            got(ref, col_r.at[f])

        chain(ref, 0, f)

        @pl.when(j == 0)
        def _():
            send(lo, lo, edge_s.at[0], edge_r.at[0], dev_x)
            send(hi, hi, edge_s.at[1], edge_r.at[1], dev_y)

    def tok_spread(j):
        f = feature_of(j)
        ref = act.at[0, f, rows(p)]
        lo, hi = act.at[0, f, rows(p, 0, half)], act.at[0, f, rows(p, half, half)]
        send(hi, hi, tx_s.at[0, j], tx_r.at[0, j], dev_x)
        send(lo, lo, ty_s.at[0, j], ty_r.at[0, j], dev_y)
        send(ref, ref, gc_s.at[0, j], gc_r.at[0, j], dev_c)

    def tok_edge(i, j):
        f = feature_of(j)
        block, first = (py, half) if i else (px, 0)
        ref = act.at[0, f, rows(block, first, half)]

        @pl.when(j == 0)
        def _():
            got(ref, edge_r.at[i])

        @pl.when(j > 0)
        def _():
            got(ref, col_r.at[8 + 4 * i + f])

        chain(ref, 2 + i, f)
        if i:
            send(ref, ref, tx_s.at[1, j], tx_r.at[1, j], dev_x)
        else:
            send(ref, ref, ty_s.at[1, j], ty_r.at[1, j], dev_y)

    def tok_near(i, j):
        f = feature_of(j)
        block, first, sem = (py, 0, ty_r) if i else (px, half, tx_r)
        got(act.at[0, f, rows(block, first, half)], sem.at[0, j])
        ref = act.at[0, f, rows(block)]
        send(ref, ref, gc_s.at[1 + i, j], gc_r.at[1 + i, j], dev_c)

    def tok_far(j):
        f = feature_of(j)
        got(act.at[0, f, rows(pd, half, half)], tx_r.at[1, j])
        got(act.at[0, f, rows(pd, 0, half)], ty_r.at[1, j])
        ref = act.at[0, f, rows(pd)]
        send(ref, ref, gc_s.at[3, j], gc_r.at[3, j], dev_c)

    def cot_own(j):
        f = feature_of(j)
        ref = act.at[1, f, rows(p)]

        @pl.when(j == 0)
        def _():
            own_dy.wait()

        @pl.when(j > 0)
        def _():
            got(ref, col_r.at[4 + f])

        chain(ref, 1, f)

    def cot_spread(j):
        ref = act.at[1, feature_of(j), rows(p)]
        send(ref, ref, gx_s.at[j], gx_r.at[j], dev_x)
        send(ref, ref, gy_s.at[j], gy_r.at[j], dev_y)
        send(ref, ref, gc_s.at[0, 4 + j], gc_r.at[0, 4 + j], dev_c)

    def cot_near(i, j):
        f = feature_of(j)
        block, sem = (py, gy_r) if i else (px, gx_r)
        ref = act.at[1, f, rows(block)]
        got(ref, sem.at[j])
        if i:
            on = act.at[1, f, rows(block, half, half)]
            send(on, on, hx_s.at[j], hx_r.at[j], dev_x)
        else:
            on = act.at[1, f, rows(block, 0, half)]
            send(on, on, hy_s.at[j], hy_r.at[j], dev_y)
        send(ref, ref, gc_s.at[1 + i, 4 + j], gc_r.at[1 + i, 4 + j], dev_c)

    def cot_far(j):
        f = feature_of(j)
        got(act.at[1, f, rows(pd, 0, half)], hy_r.at[j])
        got(act.at[1, f, rows(pd, half, half)], hx_r.at[j])
        ref = act.at[1, f, rows(pd)]
        send(ref, ref, gc_s.at[3, 4 + j], gc_r.at[3, 4 + j], dev_c)

    ET = 64

    def after_x(qi):
        q = q_of(qi)

        @pl.loop(0, 2 * H // ET)
        def _(n):
            e = lax.div(n, H // ET)
            prow = jnp.concatenate(
                [pt[2 * q, pl.ds(2 * p + e, 1), :], pt[2 * q + 1, pl.ds(2 * p + e, 1), :]], axis=1
            )
            a = pl.ds(pl.multiple_of(n * ET, ET), ET)
            b = pl.ds(pl.multiple_of(2 * H + n * ET, ET), ET)
            g, u = acc[qi, a, :], acc[qi, b, :]
            s = jax.nn.sigmoid(g)
            active = g * s
            gh[pl.ds(pl.multiple_of(4 * H + n * ET, ET), ET), cols(q)] = (
                active * u * prow
            ).astype(BF16)
            acc[qi, a, :] = u * s * (1.0 + g * (1.0 - s)) * prow
            acc[qi, b, :] = active * prow

    def after_dy(qi):
        q = q_of(qi)

        @pl.loop(0, 2)
        def _(e):
            for kind in range(2):
                lo = kind * 2 * H
                back = acc[qi, pl.ds(pl.multiple_of(4 * H + e * H, H), H), :]
                at = pl.ds(pl.multiple_of(lo + e * H, H), H)
                v = back * acc[qi, at, :]
                gh[at, cols(q)] = v.astype(BF16)
                gT[qi, :, at] = v.T.astype(BF16)

    def forward(arr, qi, j):
        f, q = feature_of(j), q_of(qi)
        got(act.at[arr, f, rows(q * 2 + 1 - c)], gc_r.at[qi, arr * 4 + j])
        if isinstance(qi, int) and qi == 0:
            for r in (4, 5) if arr else range(4):
                w_copy(r, j).wait()
            if not arr:

                @pl.when(j == 3)
                def _():
                    for d in range(1, 8):
                        got(pt.at[lax.rem(p + 8 - d, 8)], pt_r.at[d - 1])

        @pl.loop(2 * arr, 2 + arr)
        def _(n):
            at = pl.ds(pl.multiple_of(n * 2 * H, 2 * H), 2 * H)
            d = lax.dot_general(
                wv[f, at, :], act[arr, f, cols(q), :], (((1,), (1,)), ((), ())),
                preferred_element_type=F32,
            )

            @pl.when(j == 0)
            def _():
                acc[qi, at, :] = d

            @pl.when(j > 0)
            def _():
                acc[qi, at, :] += d

        @pl.when(j == 3)
        def _():
            if arr:
                after_dy(qi)
            else:
                after_x(qi)

    def both_near(arr, j):
        @pl.loop(1, 3)
        def _(qi):
            forward(arr, qi, j)

    gather_steps = (
        (4, lambda j: forward(1, 3, j)),
        (0, tok_own),
        (0, tok_spread),
        (0, lambda j: pl.when(j == 0)(weights_and_routing)),
        (2, lambda j: forward(0, 1, j)),
        (0, lambda j: forward(0, 0, j)),
        (2, lambda j: cot_near(1, j)),
        (1, lambda j: forward(1, 0, j)),
        (3, lambda j: forward(1, 1, j)),
        (1, lambda j: tok_edge(1, j)),
        (2, lambda j: cot_near(0, j)),
        (1, lambda j: tok_near(1, j)),
        (3, cot_far),
        (3, lambda j: forward(0, 3, j)),
        (2, lambda j: forward(1, 2, j)),
        (2, tok_far),
        (1, lambda j: tok_edge(0, j)),
        (0, cot_own),
        (1, lambda j: tok_near(0, j)),
        (0, cot_spread),
        (1, lambda j: forward(0, 2, j)),
    )

    def run(steps, u):
        for lag, step in steps:
            @pl.when((u >= lag) & (u < lag + 4))
            def _():
                step(u - lag)

    def gather(buf):
        nonlocal acc
        acc = buf

        @pl.loop(0, 8)
        def _(u):
            run(gather_steps, u)

    acc = Q = None
    pl.run_scoped(gather, pltpu.VMEM((4, 6 * H, 2 * T), F32))

    def quarter_of(k):
        m = 3 - k
        z0, z1 = lax.rem(z, 2), lax.div(z, 2)
        m0, m1 = lax.rem(m, 2), lax.div(m, 2)
        return (z0 + m0 * (1 - 2 * z0)) + 2 * (z1 + m1 * (1 - 2 * z1))

    def part(qi, k):
        f, q = quarter_of(k), q_of(qi)
        Q[f, cols(q), :] = jnp.dot(
            gT[qi], wv[f, pl.ds(0, 4 * H), :], preferred_element_type=F32
        ).astype(BF16)
        send(
            Q.at[f, rows(q * 2 + 1 - c)], RC.at[k, qi],
            rc_s.at[k, qi], rc_r.at[k, qi], dev_c,
        )

    AT = 32

    def add(dst, size, *terms):
        @pl.loop(0, size // AT)
        def _(n):
            at = pl.ds(pl.multiple_of(n * AT, AT), AT)
            total = dst[at, :].astype(F32)
            for t in terms:
                total = total + t[at, :].astype(F32)
            dst[at, :] = total.astype(BF16)

    def core_sum(qi, k):
        f = quarter_of(k)
        got(RC.at[k, qi], rc_r.at[k, qi])
        add(Q.at[f, rows(block_of(qi))], T, RC.at[k, qi])
        lo = Q.at[f, rows(block_of(qi), 0, half)]
        hi = Q.at[f, rows(block_of(qi), half, half)]
        if qi == 1:
            send(lo, RX.at[0, k], rx_s.at[0, k], rx_r.at[0, k], dev_x)
        elif qi == 2:
            send(hi, RY.at[0, k], ry_s.at[0, k], ry_r.at[0, k], dev_y)
        elif qi == 3:
            send(lo, RX.at[1, k], rx_s.at[1, k], rx_r.at[1, k], dev_x)
            send(hi, RY.at[1, k], ry_s.at[1, k], ry_r.at[1, k], dev_y)

    def turn_sums(k):
        f = quarter_of(k)
        got(RX.at[1, k], rx_r.at[1, k])
        lo = Q.at[f, rows(py, 0, half)]
        add(lo, half, RX.at[1, k])
        send(lo, RY.at[2, k], ry_s.at[2, k], ry_r.at[2, k], dev_y)
        got(RY.at[1, k], ry_r.at[1, k])
        hi = Q.at[f, rows(px, half, half)]
        add(hi, half, RY.at[1, k])
        send(hi, RX.at[2, k], rx_s.at[2, k], rx_r.at[2, k], dev_x)

    def plane_sums(k):
        f = quarter_of(k)
        got(RX.at[0, k], rx_r.at[0, k])
        got(RY.at[2, k], ry_r.at[2, k])
        add(Q.at[f, rows(p, 0, half)], half, RX.at[0, k], RY.at[2, k])
        got(RY.at[0, k], ry_r.at[0, k])
        got(RX.at[2, k], rx_r.at[2, k])
        add(Q.at[f, rows(p, half, half)], half, RY.at[0, k], RX.at[2, k])

        @pl.when(k < 3)
        def _():
            i = 2 - k
            send(Q.at[f, rows(p)], RZ.at[i], rz_s.at[i], rz_r.at[i], (f, p))

    def weight_grad(t):
        f, r = lax.div(t, 6), lax.rem(t, 6)
        gw_ref[r, :, pl.ds(pl.multiple_of(f * FC, FC), FC)] = jnp.dot(
            gh[pl.ds(pl.multiple_of(r * H, H), H), :], act[lax.div(r, 4), f],
            preferred_element_type=F32,
        ).astype(BF16)

    return_steps = (
        (0, lambda k: part(3, k)),
        (1, turn_sums),
        (0, lambda k: part(2, k)),
        (0, lambda k: part(1, k)),
        (0, lambda k: core_sum(3, k)),
        (1, lambda k: core_sum(0, k)),
    )
    more_return_steps = (
        (0, lambda k: core_sum(2, k)),
        (0, lambda k: core_sum(1, k)),
    )
    last_return_steps = (
        (1, plane_sums),
        (0, lambda k: part(0, k)),
    )

    def all_sent():
        for d in range(1, 8):
            got(pt.at[p], pt_s.at[d - 1])

        def sent_along(i, f):
            ref = act.at[0, f, rows(p)] if i < 2 else act.at[0, f, rows(p, 0, half)]

            @pl.when((f <= z) & (z < 3))
            def _():
                got(ref, up_s.at[i * 4 + f])

            @pl.when((f >= z) & (z > 0))
            def _():
                got(ref, dn_s.at[i * 4 + f])

        part_ref = act.at[0, 0, rows(p, 0, half)]
        got(part_ref, edge_s.at[0])
        got(part_ref, edge_s.at[1])

        @pl.loop(0, 4)
        def _(j):
            for i in range(4):
                sent_along(i, j)
            for i in range(2):
                got(part_ref, tx_s.at[i, j])
                got(part_ref, ty_s.at[i, j])
            ref = act.at[0, 0, rows(p)]
            got(ref, gx_s.at[j])
            got(ref, gy_s.at[j])
            got(part_ref, hx_s.at[j])
            got(part_ref, hy_s.at[j])
            for i in range(4):
                got(ref, gc_s.at[i, j])
                got(ref, gc_s.at[i, 4 + j])

        @pl.loop(0, 4)
        def _(k):
            @pl.loop(0, 4)
            def _(qi):
                got(RC.at[k, qi], rc_s.at[k, qi])

            for i in range(3):
                got(RX.at[i, k], rx_s.at[i, k])
                got(RY.at[i, k], ry_s.at[i, k])

    def give_back(buf):
        nonlocal Q
        Q = buf

        @pl.loop(0, 5)
        def _(u):
            run(return_steps, u)

            @pl.loop(0, 3)
            def _(n):
                weight_grad(u * 5 + n)

            run(more_return_steps, u)

            @pl.loop(3, 5 - lax.div(u, 4))
            def _(n):
                weight_grad(u * 5 + n)

            run(last_return_steps, u)

        all_sent()
        for i in range(3):
            got(RZ.at[i], rz_r.at[i])

        @pl.loop(0, T // AT)
        def _(n):
            at = pl.ds(pl.multiple_of(n * AT, AT), AT)
            total = Q[z, pl.ds(pl.multiple_of(p * T + n * AT, AT), AT), :].astype(F32)
            for i in range(3):
                total = total + RZ[i, at, :].astype(F32)
            gt_ref[at, :] = total.astype(BF16)

        for i in range(3):
            got(RZ.at[i], rz_s.at[i])

    pl.run_scoped(give_back, pltpu.VMEM((4, act.shape[2], FC), BF16))


def to_hbm_kernel(gt_ref, gw_ref, gt_out, gate_out, up_out, down_out, sem):
    copies = [pltpu.make_async_copy(gt_ref, gt_out, sem.at[6])]
    for r in range(6):
        out = (gate_out, up_out, down_out)[r // 2]
        copies.append(pltpu.make_async_copy(gw_ref.at[r], out.at[r % 2], sem.at[r]))
    for c in copies:
        c.start()
    for c in copies:
        c.wait()


def dense_body(tokens, grad_out, expert_ids, route_prob, w_gate, w_up, w_down):
    T, FC = tokens.shape
    E, H, D = w_gate.shape
    blocks = lax.axis_size("expert")
    N = blocks * T
    experts = blocks * E
    dma = pltpu.SemaphoreType.DMA
    any_ = pl.BlockSpec(memory_space=pl.ANY)
    vmem = pl.BlockSpec(memory_space=pltpu.VMEM)
    grad_tokens, gw = pl.pallas_call(
        dense_kernel,
        out_shape=(pltpu.VMEM((T, FC), BF16), pltpu.VMEM((3 * E, H, D), BF16)),
        in_specs=[any_, any_, vmem, vmem, any_, any_, any_],
        out_specs=(vmem, vmem),
        scratch_shapes=[
            pltpu.VMEM((2, 4, N, FC), BF16),
            pltpu.VMEM((4, 6 * H, FC), BF16),
            pltpu.VMEM((6 * H, N), BF16),
            pltpu.VMEM((4, 2 * T, 4 * H), BF16),
            pltpu.VMEM((4, 4, T, FC), BF16),
            pltpu.VMEM((3, 4, T // 2, FC), BF16),
            pltpu.VMEM((3, 4, T // 2, FC), BF16),
            pltpu.VMEM((3, T, FC), BF16),
            pltpu.VMEM((blocks, experts, 128), F32),
            dma((6, 4)), dma((2,)), dma((7,)), dma((7,)),
            dma((16,)), dma((16,)), dma((16,)), dma((2,)), dma((2,)),
            dma((2, 4)), dma((2, 4)), dma((2, 4)), dma((2, 4)),
            dma((4,)), dma((4,)), dma((4,)), dma((4,)),
            dma((4,)), dma((4,)), dma((4,)), dma((4,)),
            dma((4, 8)), dma((4, 8)), dma((4, 4)), dma((4, 4)),
            dma((3, 4)), dma((3, 4)), dma((3, 4)), dma((3, 4)),
            dma((3,)), dma((3,)),
        ],
        compiler_params=pltpu.CompilerParams(
            collective_id=0, has_side_effects=True, vmem_limit_bytes=51 << 20
        ),
        cost_estimate=pl.CostEstimate(
            flops=2 * N * D * 16 * H, bytes_accessed=12 * E * H * D, transcendentals=N * E * H
        ),
    )(tokens, grad_out, expert_ids.T, route_prob.T, w_gate, w_up, w_down)
    grad_w = jax.ShapeDtypeStruct((E, H, D), BF16)
    return pl.pallas_call(
        to_hbm_kernel,
        out_shape=(jax.ShapeDtypeStruct((T, FC), BF16), grad_w, grad_w, grad_w),
        in_specs=[any_, any_],
        out_specs=(any_,) * 4,
        scratch_shapes=[dma((7,))],
        compiler_params=pltpu.CompilerParams(vmem_limit_bytes=1 << 20),
    )(grad_tokens, gw)


def solution(mesh):
    placed = (
        P("expert", "edata"),
        P("expert", "edata"),
        P("expert", None),
        P("expert", None),
        P("expert", "edata", None),
        P("expert", "edata", None),
        P("expert", "edata", None),
    )
    small = mesh.shape["expert"] == 8 and mesh.shape["edata"] == 4
    return jax.shard_map(
        dense_body if small else slots_body,
        mesh=mesh,
        in_specs=placed,
        out_specs=(
            P("expert", "edata"),
            P("expert", "edata", None),
            P("expert", "edata", None),
            P("expert", "edata", None),
        ),
        check_vma=False,
    )
```

```python
import jax
import jax.numpy as jnp
from jax import lax
from jax.experimental import pallas as pl
from jax.experimental.pallas import tpu as pltpu
from jax.sharding import PartitionSpec as P

MESH = pl.DeviceIdType.MESH
BF16 = jnp.bfloat16
F32 = jnp.float32


def ranks(onehot):
    pair_count = onehot.shape[-2]
    row = lax.broadcasted_iota(jnp.int32, (pair_count, pair_count), 0)
    col = lax.broadcasted_iota(jnp.int32, (pair_count, pair_count), 1)
    tri = (col < row).astype(jnp.bfloat16)
    earlier = jnp.einsum(
        "pq,...qe->...pe", tri, onehot.astype(jnp.bfloat16), preferred_element_type=jnp.float32
    )
    return earlier.astype(jnp.int32)


def slots_body(tokens, grad_out, expert_ids, route_prob, w_gate, w_up, w_down):
    token_count, top_count = expert_ids.shape
    local_experts = w_gate.shape[0]
    expert_devices = lax.axis_size("expert")
    me = lax.axis_index("expert")
    experts_all = expert_devices * local_experts
    capacity = token_count * top_count * 5 // (4 * experts_all)
    pair_count = token_count * top_count
    cap_iota = jnp.arange(capacity, dtype=jnp.int32)

    routing = jnp.stack([expert_ids.astype(jnp.float32), route_prob])
    routing = lax.all_gather(routing, "expert", axis=1, tiled=False)
    all_ids, all_prob = routing[0].astype(jnp.int32), routing[1]
    mine = me * local_experts + jnp.arange(local_experts, dtype=jnp.int32)
    named = all_ids.reshape(expert_devices, pair_count)[:, :, None] == mine
    rank = ranks(named)
    hit = named[..., None] & (rank[..., None] == cap_iota)
    hit = hit.reshape(expert_devices, token_count, top_count, local_experts, capacity)
    pick = jnp.sum(hit.astype(jnp.int32), 2).astype(jnp.bfloat16)
    prob_of = jnp.sum(jnp.where(hit, all_prob[:, :, :, None, None], 0.0), (1, 2))

    both = lax.all_gather(jnp.stack([tokens, grad_out]), "edata", axis=2, tiled=True)
    both = lax.all_gather(both, "expert", axis=1, tiled=False)
    all_x, all_dy = both[0], both[1]
    slot_x = jnp.einsum(
        "stxc,std->sxcd", pick, all_x, preferred_element_type=jnp.float32
    ).astype(jnp.bfloat16)
    slot_dy = jnp.einsum("stxc,std->sxcd", pick, all_dy, preferred_element_type=jnp.float32)
    slot_dy = (prob_of[..., None] * slot_dy).astype(jnp.bfloat16)

    gate_value = jnp.einsum("sxcd,xfd->sxcf", slot_x, w_gate, preferred_element_type=jnp.float32)
    up_value = jnp.einsum("sxcd,xfd->sxcf", slot_x, w_up, preferred_element_type=jnp.float32)
    sigma = jax.nn.sigmoid(gate_value)
    active = gate_value * sigma
    hidden = (active * up_value).astype(jnp.bfloat16)
    back = jnp.einsum("sxcd,xfd->sxcf", slot_dy, w_down, preferred_element_type=jnp.float32)
    gate_grad = (back * up_value * sigma * (1.0 + gate_value * (1.0 - sigma))).astype(jnp.bfloat16)
    up_grad = (back * active).astype(jnp.bfloat16)
    grad_gate = jnp.einsum(
        "sxcf,sxcd->xfd", gate_grad, slot_x, preferred_element_type=jnp.float32
    ).astype(jnp.bfloat16)
    grad_up = jnp.einsum(
        "sxcf,sxcd->xfd", up_grad, slot_x, preferred_element_type=jnp.float32
    ).astype(jnp.bfloat16)
    grad_down = jnp.einsum(
        "sxcf,sxcd->xfd", hidden, slot_dy, preferred_element_type=jnp.float32
    ).astype(jnp.bfloat16)
    partial_value = jnp.einsum(
        "sxcf,xfd->sxcd", gate_grad, w_gate, preferred_element_type=jnp.float32
    )
    partial_value = partial_value + jnp.einsum(
        "sxcf,xfd->sxcd", up_grad, w_up, preferred_element_type=jnp.float32
    )
    partial_value = partial_value.astype(jnp.bfloat16)
    returned = lax.all_to_all(
        partial_value.reshape(expert_devices, local_experts * capacity, -1),
        "expert",
        split_axis=0,
        concat_axis=0,
        tiled=True,
    )
    width = returned.shape[-1]

    own = expert_ids.reshape(pair_count, 1) == jnp.arange(experts_all, dtype=jnp.int32)
    slot = jnp.sum(jnp.where(own, ranks(own), 0), 1)
    back_hit = own[:, :, None] & (slot[:, None, None] == cap_iota)
    gather_back = jnp.sum(
        back_hit.reshape(token_count, top_count, experts_all * capacity).astype(jnp.int32), 1
    ).astype(jnp.bfloat16)
    per_token = jnp.einsum(
        "tq,qd->td",
        gather_back,
        returned.reshape(experts_all * capacity, width),
        preferred_element_type=jnp.float32,
    )
    grad_tokens = lax.psum_scatter(per_token, "edata", scatter_dimension=1, tiled=True).astype(
        jnp.bfloat16
    )
    return (grad_tokens, grad_gate, grad_up, grad_down)


def dense_kernel(
    tokens_ref, dy_ref, ids_ref, prob_ref, wg_ref, wu_ref, wd_ref,
    gt_ref, gw_ref,
    act, wv, gh, gT, RC, RX, RY, RZ, pt,
    w_sem, own_sem, pt_s, pt_r, up_s, dn_s, col_r, edge_s, edge_r, tx_s, tx_r, ty_s, ty_r,
    gx_s, gx_r, gy_s, gy_r, hx_s, hx_r, hy_s, hy_r, gc_s, gc_r, rc_s, rc_r, rx_s, rx_r, ry_s, ry_r,
    rz_s, rz_r,
):
    T, FC = tokens_ref.shape
    H = wg_ref.shape[1]
    half = T // 2
    z = lax.axis_index("edata")
    p = lax.axis_index("expert")
    c = lax.rem(p, 2)
    x = lax.rem(lax.div(p, 2), 2)
    y = lax.div(p, 4)

    def q_of(qi):
        a, b = qi % 2, qi // 2
        if not isinstance(qi, int):
            a, b = lax.rem(qi, 2), lax.div(qi, 2)
        return (y + b * (1 - 2 * y)) * 2 + (x + a * (1 - 2 * x))

    def block_of(qi):
        return q_of(qi) * 2 + c

    px, py, pd, pc = block_of(1), block_of(2), block_of(3), q_of(0) * 2 + 1 - c
    dev_x, dev_y, dev_c = (z, px), (z, py), (z, pc)

    def rows(block, first=0, size=T):
        return pl.ds(pl.multiple_of(block * T + first, half), size)

    def cols(q):
        return pl.ds(pl.multiple_of(q * 2 * T, 2 * T), 2 * T)

    def feature_of(j):
        hi = lax.div(z, 2)
        zz = hi * (3 - z) + (1 - hi) * z
        near = jnp.where(j == 0, zz, 1 - zz)
        g = jnp.where(j < 2, near, j)
        return hi * (3 - g) + (1 - hi) * g

    def send(src, dst, s_sem, r_sem, dev):
        pltpu.make_async_remote_copy(
            src_ref=src, dst_ref=dst, send_sem=s_sem, recv_sem=r_sem,
            device_id=dev, device_id_type=MESH,
        ).start()

    def got(dst, sem):
        pltpu.make_async_copy(dst, dst, sem).wait()

    bar = pltpu.get_barrier_semaphore()
    for d in range(1, 8):
        pl.semaphore_signal(bar, inc=1, device_id=(z, lax.rem(p + d, 8)), device_id_type=MESH)
    for d in range(1, 4):
        pl.semaphore_signal(bar, inc=1, device_id=(lax.rem(z + d, 4), p), device_id_type=MESH)
    own_x = pltpu.make_async_copy(tokens_ref, act.at[0, z, rows(p)], own_sem.at[0])
    own_dy = pltpu.make_async_copy(dy_ref, act.at[1, z, rows(p)], own_sem.at[1])
    own_x.start()
    own_dy.start()
    wrefs = (wg_ref, wu_ref, wd_ref)

    def w_copy(r, j):
        f = feature_of(j)
        return pltpu.make_async_copy(
            wrefs[r // 2].at[r % 2, :, pl.ds(pl.multiple_of(f * FC, FC), FC)],
            wv.at[f, pl.ds(r * H, H), :],
            w_sem.at[r, j],
        )

    def weights_and_routing():
        for j in range(4):
            for r in range(6):
                w_copy(r, j).start()
        ids, prob = ids_ref[...], prob_ref[...]
        pt[p] = jnp.concatenate(
            [
                jnp.sum(jnp.where(ids == e, prob, 0.0), axis=0, keepdims=True)
                for e in range(pt.shape[1])
            ],
            axis=0,
        )
        for d in range(1, 8):
            send(pt.at[p], pt.at[p], pt_s.at[d - 1], pt_r.at[d - 1], (z, lax.rem(p + d, 8)))

    pl.semaphore_wait(bar, 10)

    def chain(ref, i, f):
        i = i * 4 + f

        @pl.when((f <= z) & (z < 3))
        def _():
            send(ref, ref, up_s.at[i], col_r.at[i], (z + 1, p))

        @pl.when((f >= z) & (z > 0))
        def _():
            send(ref, ref, dn_s.at[i], col_r.at[i], (z - 1, p))

    def tok_own(j):
        f = feature_of(j)
        ref = act.at[0, f, rows(p)]
        lo, hi = act.at[0, f, rows(p, 0, half)], act.at[0, f, rows(p, half, half)]

        @pl.when(j == 0)
        def _():
            own_x.wait()

        @pl.when(j > 0)
        def _():
            got(ref, col_r.at[f])

        chain(ref, 0, f)

        @pl.when(j == 0)
        def _():
            send(lo, lo, edge_s.at[0], edge_r.at[0], dev_x)
            send(hi, hi, edge_s.at[1], edge_r.at[1], dev_y)

    def tok_spread(j):
        f = feature_of(j)
        ref = act.at[0, f, rows(p)]
        lo, hi = act.at[0, f, rows(p, 0, half)], act.at[0, f, rows(p, half, half)]
        send(hi, hi, tx_s.at[0, j], tx_r.at[0, j], dev_x)
        send(lo, lo, ty_s.at[0, j], ty_r.at[0, j], dev_y)
        send(ref, ref, gc_s.at[0, j], gc_r.at[0, j], dev_c)

    def tok_edge(i, j):
        f = feature_of(j)
        block, first = (py, half) if i else (px, 0)
        ref = act.at[0, f, rows(block, first, half)]

        @pl.when(j == 0)
        def _():
            got(ref, edge_r.at[i])

        @pl.when(j > 0)
        def _():
            got(ref, col_r.at[8 + 4 * i + f])

        chain(ref, 2 + i, f)
        if i:
            send(ref, ref, tx_s.at[1, j], tx_r.at[1, j], dev_x)
        else:
            send(ref, ref, ty_s.at[1, j], ty_r.at[1, j], dev_y)

    def tok_near(i, j):
        f = feature_of(j)
        block, first, sem = (py, 0, ty_r) if i else (px, half, tx_r)
        got(act.at[0, f, rows(block, first, half)], sem.at[0, j])
        ref = act.at[0, f, rows(block)]
        send(ref, ref, gc_s.at[1 + i, j], gc_r.at[1 + i, j], dev_c)

    def tok_far(j):
        f = feature_of(j)
        got(act.at[0, f, rows(pd, half, half)], tx_r.at[1, j])
        got(act.at[0, f, rows(pd, 0, half)], ty_r.at[1, j])
        ref = act.at[0, f, rows(pd)]
        send(ref, ref, gc_s.at[3, j], gc_r.at[3, j], dev_c)

    def cot_own(j):
        f = feature_of(j)
        ref = act.at[1, f, rows(p)]

        @pl.when(j == 0)
        def _():
            own_dy.wait()

        @pl.when(j > 0)
        def _():
            got(ref, col_r.at[4 + f])

        chain(ref, 1, f)

    def cot_spread(j):
        ref = act.at[1, feature_of(j), rows(p)]
        send(ref, ref, gx_s.at[j], gx_r.at[j], dev_x)
        send(ref, ref, gy_s.at[j], gy_r.at[j], dev_y)
        send(ref, ref, gc_s.at[0, 4 + j], gc_r.at[0, 4 + j], dev_c)

    def cot_near(i, j):
        f = feature_of(j)
        block, sem = (py, gy_r) if i else (px, gx_r)
        ref = act.at[1, f, rows(block)]
        got(ref, sem.at[j])
        if i:
            on = act.at[1, f, rows(block, half, half)]
            send(on, on, hx_s.at[j], hx_r.at[j], dev_x)
        else:
            on = act.at[1, f, rows(block, 0, half)]
            send(on, on, hy_s.at[j], hy_r.at[j], dev_y)
        send(ref, ref, gc_s.at[1 + i, 4 + j], gc_r.at[1 + i, 4 + j], dev_c)

    def cot_far(j):
        f = feature_of(j)
        got(act.at[1, f, rows(pd, 0, half)], hy_r.at[j])
        got(act.at[1, f, rows(pd, half, half)], hx_r.at[j])
        ref = act.at[1, f, rows(pd)]
        send(ref, ref, gc_s.at[3, 4 + j], gc_r.at[3, 4 + j], dev_c)

    ET = 64

    def after_x(qi):
        q = q_of(qi)

        @pl.loop(0, 2 * H // ET)
        def _(n):
            e = lax.div(n, H // ET)
            prow = jnp.concatenate(
                [pt[2 * q, pl.ds(2 * p + e, 1), :], pt[2 * q + 1, pl.ds(2 * p + e, 1), :]], axis=1
            )
            a = pl.ds(pl.multiple_of(n * ET, ET), ET)
            b = pl.ds(pl.multiple_of(2 * H + n * ET, ET), ET)
            g, u = acc[qi, a, :], acc[qi, b, :]
            s = jax.nn.sigmoid(g)
            active = g * s
            gh[pl.ds(pl.multiple_of(4 * H + n * ET, ET), ET), cols(q)] = (
                active * u * prow
            ).astype(BF16)
            acc[qi, a, :] = u * s * (1.0 + g * (1.0 - s)) * prow
            acc[qi, b, :] = active * prow

    def after_dy(qi):
        q = q_of(qi)

        @pl.loop(0, 2)
        def _(e):
            for kind in range(2):
                lo = kind * 2 * H
                back = acc[qi, pl.ds(pl.multiple_of(4 * H + e * H, H), H), :]
                at = pl.ds(pl.multiple_of(lo + e * H, H), H)
                v = back * acc[qi, at, :]
                gh[at, cols(q)] = v.astype(BF16)
                gT[qi, :, at] = v.T.astype(BF16)

    def forward(arr, qi, j):
        f, q = feature_of(j), q_of(qi)
        got(act.at[arr, f, rows(q * 2 + 1 - c)], gc_r.at[qi, arr * 4 + j])
        if isinstance(qi, int) and qi == 0:
            for r in (4, 5) if arr else range(4):
                w_copy(r, j).wait()
            if not arr:

                @pl.when(j == 3)
                def _():
                    for d in range(1, 8):
                        got(pt.at[lax.rem(p + 8 - d, 8)], pt_r.at[d - 1])

        @pl.loop(2 * arr, 2 + arr)
        def _(n):
            at = pl.ds(pl.multiple_of(n * 2 * H, 2 * H), 2 * H)
            d = lax.dot_general(
                wv[f, at, :], act[arr, f, cols(q), :], (((1,), (1,)), ((), ())),
                preferred_element_type=F32,
            )

            @pl.when(j == 0)
            def _():
                acc[qi, at, :] = d

            @pl.when(j > 0)
            def _():
                acc[qi, at, :] += d

        @pl.when(j == 3)
        def _():
            if arr:
                after_dy(qi)
            else:
                after_x(qi)

    def both_near(arr, j):
        @pl.loop(1, 3)
        def _(qi):
            forward(arr, qi, j)

    def cot_first(j):
        @pl.when(j == 0)
        def _():
            cot_own(j)
            cot_spread(j)

    def cot_later(j):
        @pl.when(j > 0)
        def _():
            cot_own(j)

    def cot_later_spread(j):
        @pl.when(j > 0)
        def _():
            cot_spread(j)

    gather_steps = (
        (4, lambda j: forward(1, 3, j)),
        (0, tok_own),
        (0, tok_spread),
        (0, lambda j: pl.when(j == 0)(weights_and_routing)),
        (2, lambda j: forward(0, 1, j)),
        (0, cot_first),
        (0, lambda j: forward(0, 0, j)),
        (2, lambda j: cot_near(1, j)),
        (1, lambda j: forward(1, 0, j)),
        (3, lambda j: forward(1, 1, j)),
        (1, lambda j: tok_edge(1, j)),
        (2, lambda j: cot_near(0, j)),
        (1, lambda j: tok_near(1, j)),
        (3, cot_far),
        (3, lambda j: forward(0, 3, j)),
        (2, lambda j: forward(1, 2, j)),
        (2, tok_far),
        (1, lambda j: tok_edge(0, j)),
        (0, cot_later),
        (1, lambda j: tok_near(0, j)),
        (0, cot_later_spread),
        (1, lambda j: forward(0, 2, j)),
    )

    def run(steps, u):
        for lag, step in steps:
            @pl.when((u >= lag) & (u < lag + 4))
            def _():
                step(u - lag)

    def gather(buf):
        nonlocal acc
        acc = buf

        @pl.loop(0, 8)
        def _(u):
            run(gather_steps, u)

    acc = Q = None
    pl.run_scoped(gather, pltpu.VMEM((4, 6 * H, 2 * T), F32))

    def quarter_of(k):
        m = 3 - k
        z0, z1 = lax.rem(z, 2), lax.div(z, 2)
        m0, m1 = lax.rem(m, 2), lax.div(m, 2)
        return (z0 + m0 * (1 - 2 * z0)) + 2 * (z1 + m1 * (1 - 2 * z1))

    def part(qi, k):
        f, q = quarter_of(k), q_of(qi)
        Q[f, cols(q), :] = jnp.dot(
            gT[qi], wv[f, pl.ds(0, 4 * H), :], preferred_element_type=F32
        ).astype(BF16)
        send(
            Q.at[f, rows(q * 2 + 1 - c)], RC.at[k, qi],
            rc_s.at[k, qi], rc_r.at[k, qi], dev_c,
        )

    AT = 32

    def add(dst, size, *terms):
        @pl.loop(0, size // AT)
        def _(n):
            at = pl.ds(pl.multiple_of(n * AT, AT), AT)
            total = dst[at, :].astype(F32)
            for t in terms:
                total = total + t[at, :].astype(F32)
            dst[at, :] = total.astype(BF16)

    def core_sum(qi, k):
        f = quarter_of(k)
        got(RC.at[k, qi], rc_r.at[k, qi])
        add(Q.at[f, rows(block_of(qi))], T, RC.at[k, qi])
        lo = Q.at[f, rows(block_of(qi), 0, half)]
        hi = Q.at[f, rows(block_of(qi), half, half)]
        if qi == 1:
            send(lo, RX.at[0, k], rx_s.at[0, k], rx_r.at[0, k], dev_x)
        elif qi == 2:
            send(hi, RY.at[0, k], ry_s.at[0, k], ry_r.at[0, k], dev_y)
        elif qi == 3:
            send(lo, RX.at[1, k], rx_s.at[1, k], rx_r.at[1, k], dev_x)
            send(hi, RY.at[1, k], ry_s.at[1, k], ry_r.at[1, k], dev_y)

    def turn_sums(k):
        f = quarter_of(k)
        got(RX.at[1, k], rx_r.at[1, k])
        lo = Q.at[f, rows(py, 0, half)]
        add(lo, half, RX.at[1, k])
        send(lo, RY.at[2, k], ry_s.at[2, k], ry_r.at[2, k], dev_y)
        got(RY.at[1, k], ry_r.at[1, k])
        hi = Q.at[f, rows(px, half, half)]
        add(hi, half, RY.at[1, k])
        send(hi, RX.at[2, k], rx_s.at[2, k], rx_r.at[2, k], dev_x)

    def plane_sums(k):
        f = quarter_of(k)
        got(RX.at[0, k], rx_r.at[0, k])
        got(RY.at[2, k], ry_r.at[2, k])
        add(Q.at[f, rows(p, 0, half)], half, RX.at[0, k], RY.at[2, k])
        got(RY.at[0, k], ry_r.at[0, k])
        got(RX.at[2, k], rx_r.at[2, k])
        add(Q.at[f, rows(p, half, half)], half, RY.at[0, k], RX.at[2, k])

        @pl.when(k < 3)
        def _():
            i = 2 - k
            send(Q.at[f, rows(p)], RZ.at[i], rz_s.at[i], rz_r.at[i], (f, p))

    def weight_grad(t):
        f, r = lax.div(t, 6), lax.rem(t, 6)
        gw_ref[r, :, pl.ds(pl.multiple_of(f * FC, FC), FC)] = jnp.dot(
            gh[pl.ds(pl.multiple_of(r * H, H), H), :], act[lax.div(r, 4), f],
            preferred_element_type=F32,
        ).astype(BF16)

    return_steps = (
        (0, lambda k: part(3, k)),
        (1, turn_sums),
        (0, lambda k: part(2, k)),
        (0, lambda k: part(1, k)),
        (0, lambda k: core_sum(3, k)),
        (1, lambda k: core_sum(0, k)),
    )
    more_return_steps = (
        (0, lambda k: core_sum(2, k)),
        (0, lambda k: core_sum(1, k)),
    )
    last_return_steps = (
        (1, plane_sums),
        (0, lambda k: part(0, k)),
    )

    def all_sent():
        for d in range(1, 8):
            got(pt.at[p], pt_s.at[d - 1])

        def sent_along(i, f):
            ref = act.at[0, f, rows(p)] if i < 2 else act.at[0, f, rows(p, 0, half)]

            @pl.when((f <= z) & (z < 3))
            def _():
                got(ref, up_s.at[i * 4 + f])

            @pl.when((f >= z) & (z > 0))
            def _():
                got(ref, dn_s.at[i * 4 + f])

        part_ref = act.at[0, 0, rows(p, 0, half)]
        got(part_ref, edge_s.at[0])
        got(part_ref, edge_s.at[1])

        @pl.loop(0, 4)
        def _(j):
            for i in range(4):
                sent_along(i, j)
            for i in range(2):
                got(part_ref, tx_s.at[i, j])
                got(part_ref, ty_s.at[i, j])
            ref = act.at[0, 0, rows(p)]
            got(ref, gx_s.at[j])
            got(ref, gy_s.at[j])
            got(part_ref, hx_s.at[j])
            got(part_ref, hy_s.at[j])
            for i in range(4):
                got(ref, gc_s.at[i, j])
                got(ref, gc_s.at[i, 4 + j])

        @pl.loop(0, 4)
        def _(k):
            @pl.loop(0, 4)
            def _(qi):
                got(RC.at[k, qi], rc_s.at[k, qi])

            for i in range(3):
                got(RX.at[i, k], rx_s.at[i, k])
                got(RY.at[i, k], ry_s.at[i, k])

    def give_back(buf):
        nonlocal Q
        Q = buf

        @pl.loop(0, 5)
        def _(u):
            run(return_steps, u)

            @pl.loop(0, 3)
            def _(n):
                weight_grad(u * 5 + n)

            run(more_return_steps, u)

            @pl.loop(3, 5 - lax.div(u, 4))
            def _(n):
                weight_grad(u * 5 + n)

            run(last_return_steps, u)

        all_sent()
        for i in range(3):
            got(RZ.at[i], rz_r.at[i])

        @pl.loop(0, T // AT)
        def _(n):
            at = pl.ds(pl.multiple_of(n * AT, AT), AT)
            total = Q[z, pl.ds(pl.multiple_of(p * T + n * AT, AT), AT), :].astype(F32)
            for i in range(3):
                total = total + RZ[i, at, :].astype(F32)
            gt_ref[at, :] = total.astype(BF16)

        for i in range(3):
            got(RZ.at[i], rz_s.at[i])

    pl.run_scoped(give_back, pltpu.VMEM((4, act.shape[2], FC), BF16))


def to_hbm_kernel(gt_ref, gw_ref, gt_out, gate_out, up_out, down_out, sem):
    copies = [pltpu.make_async_copy(gt_ref, gt_out, sem.at[6])]
    for r in range(6):
        out = (gate_out, up_out, down_out)[r // 2]
        copies.append(pltpu.make_async_copy(gw_ref.at[r], out.at[r % 2], sem.at[r]))
    for c in copies:
        c.start()
    for c in copies:
        c.wait()


def dense_body(tokens, grad_out, expert_ids, route_prob, w_gate, w_up, w_down):
    T, FC = tokens.shape
    E, H, D = w_gate.shape
    blocks = lax.axis_size("expert")
    N = blocks * T
    experts = blocks * E
    dma = pltpu.SemaphoreType.DMA
    any_ = pl.BlockSpec(memory_space=pl.ANY)
    vmem = pl.BlockSpec(memory_space=pltpu.VMEM)
    grad_tokens, gw = pl.pallas_call(
        dense_kernel,
        out_shape=(pltpu.VMEM((T, FC), BF16), pltpu.VMEM((3 * E, H, D), BF16)),
        in_specs=[any_, any_, vmem, vmem, any_, any_, any_],
        out_specs=(vmem, vmem),
        scratch_shapes=[
            pltpu.VMEM((2, 4, N, FC), BF16),
            pltpu.VMEM((4, 6 * H, FC), BF16),
            pltpu.VMEM((6 * H, N), BF16),
            pltpu.VMEM((4, 2 * T, 4 * H), BF16),
            pltpu.VMEM((4, 4, T, FC), BF16),
            pltpu.VMEM((3, 4, T // 2, FC), BF16),
            pltpu.VMEM((3, 4, T // 2, FC), BF16),
            pltpu.VMEM((3, T, FC), BF16),
            pltpu.VMEM((blocks, experts, 128), F32),
            dma((6, 4)), dma((2,)), dma((7,)), dma((7,)),
            dma((16,)), dma((16,)), dma((16,)), dma((2,)), dma((2,)),
            dma((2, 4)), dma((2, 4)), dma((2, 4)), dma((2, 4)),
            dma((4,)), dma((4,)), dma((4,)), dma((4,)),
            dma((4,)), dma((4,)), dma((4,)), dma((4,)),
            dma((4, 8)), dma((4, 8)), dma((4, 4)), dma((4, 4)),
            dma((3, 4)), dma((3, 4)), dma((3, 4)), dma((3, 4)),
            dma((3,)), dma((3,)),
        ],
        compiler_params=pltpu.CompilerParams(
            collective_id=0, has_side_effects=True, vmem_limit_bytes=51 << 20
        ),
        cost_estimate=pl.CostEstimate(
            flops=2 * N * D * 16 * H, bytes_accessed=12 * E * H * D, transcendentals=N * E * H
        ),
    )(tokens, grad_out, expert_ids.T, route_prob.T, w_gate, w_up, w_down)
    grad_w = jax.ShapeDtypeStruct((E, H, D), BF16)
    return pl.pallas_call(
        to_hbm_kernel,
        out_shape=(jax.ShapeDtypeStruct((T, FC), BF16), grad_w, grad_w, grad_w),
        in_specs=[any_, any_],
        out_specs=(any_,) * 4,
        scratch_shapes=[dma((7,))],
        compiler_params=pltpu.CompilerParams(vmem_limit_bytes=1 << 20),
    )(grad_tokens, gw)


def solution(mesh):
    placed = (
        P("expert", "edata"),
        P("expert", "edata"),
        P("expert", None),
        P("expert", None),
        P("expert", "edata", None),
        P("expert", "edata", None),
        P("expert", "edata", None),
    )
    small = mesh.shape["expert"] == 8 and mesh.shape["edata"] == 4
    return jax.shard_map(
        dense_body if small else slots_body,
        mesh=mesh,
        in_specs=placed,
        out_specs=(
            P("expert", "edata"),
            P("expert", "edata", None),
            P("expert", "edata", None),
            P("expert", "edata", None),
        ),
        check_vma=False,
    )
```

```python
import jax
import jax.numpy as jnp
from jax import lax
from jax.experimental import pallas as pl
from jax.experimental.pallas import tpu as pltpu
from jax.sharding import PartitionSpec as P

MESH = pl.DeviceIdType.MESH
BF16 = jnp.bfloat16
F32 = jnp.float32


def ranks(onehot):
    pair_count = onehot.shape[-2]
    row = lax.broadcasted_iota(jnp.int32, (pair_count, pair_count), 0)
    col = lax.broadcasted_iota(jnp.int32, (pair_count, pair_count), 1)
    tri = (col < row).astype(jnp.bfloat16)
    earlier = jnp.einsum(
        "pq,...qe->...pe", tri, onehot.astype(jnp.bfloat16), preferred_element_type=jnp.float32
    )
    return earlier.astype(jnp.int32)


def slots_body(tokens, grad_out, expert_ids, route_prob, w_gate, w_up, w_down):
    token_count, top_count = expert_ids.shape
    local_experts = w_gate.shape[0]
    expert_devices = lax.axis_size("expert")
    me = lax.axis_index("expert")
    experts_all = expert_devices * local_experts
    capacity = token_count * top_count * 5 // (4 * experts_all)
    pair_count = token_count * top_count
    cap_iota = jnp.arange(capacity, dtype=jnp.int32)

    routing = jnp.stack([expert_ids.astype(jnp.float32), route_prob])
    routing = lax.all_gather(routing, "expert", axis=1, tiled=False)
    all_ids, all_prob = routing[0].astype(jnp.int32), routing[1]
    mine = me * local_experts + jnp.arange(local_experts, dtype=jnp.int32)
    named = all_ids.reshape(expert_devices, pair_count)[:, :, None] == mine
    rank = ranks(named)
    hit = named[..., None] & (rank[..., None] == cap_iota)
    hit = hit.reshape(expert_devices, token_count, top_count, local_experts, capacity)
    pick = jnp.sum(hit.astype(jnp.int32), 2).astype(jnp.bfloat16)
    prob_of = jnp.sum(jnp.where(hit, all_prob[:, :, :, None, None], 0.0), (1, 2))

    both = lax.all_gather(jnp.stack([tokens, grad_out]), "edata", axis=2, tiled=True)
    both = lax.all_gather(both, "expert", axis=1, tiled=False)
    all_x, all_dy = both[0], both[1]
    slot_x = jnp.einsum(
        "stxc,std->sxcd", pick, all_x, preferred_element_type=jnp.float32
    ).astype(jnp.bfloat16)
    slot_dy = jnp.einsum("stxc,std->sxcd", pick, all_dy, preferred_element_type=jnp.float32)
    slot_dy = (prob_of[..., None] * slot_dy).astype(jnp.bfloat16)

    gate_value = jnp.einsum("sxcd,xfd->sxcf", slot_x, w_gate, preferred_element_type=jnp.float32)
    up_value = jnp.einsum("sxcd,xfd->sxcf", slot_x, w_up, preferred_element_type=jnp.float32)
    sigma = jax.nn.sigmoid(gate_value)
    active = gate_value * sigma
    hidden = (active * up_value).astype(jnp.bfloat16)
    back = jnp.einsum("sxcd,xfd->sxcf", slot_dy, w_down, preferred_element_type=jnp.float32)
    gate_grad = (back * up_value * sigma * (1.0 + gate_value * (1.0 - sigma))).astype(jnp.bfloat16)
    up_grad = (back * active).astype(jnp.bfloat16)
    grad_gate = jnp.einsum(
        "sxcf,sxcd->xfd", gate_grad, slot_x, preferred_element_type=jnp.float32
    ).astype(jnp.bfloat16)
    grad_up = jnp.einsum(
        "sxcf,sxcd->xfd", up_grad, slot_x, preferred_element_type=jnp.float32
    ).astype(jnp.bfloat16)
    grad_down = jnp.einsum(
        "sxcf,sxcd->xfd", hidden, slot_dy, preferred_element_type=jnp.float32
    ).astype(jnp.bfloat16)
    partial_value = jnp.einsum(
        "sxcf,xfd->sxcd", gate_grad, w_gate, preferred_element_type=jnp.float32
    )
    partial_value = partial_value + jnp.einsum(
        "sxcf,xfd->sxcd", up_grad, w_up, preferred_element_type=jnp.float32
    )
    partial_value = partial_value.astype(jnp.bfloat16)
    returned = lax.all_to_all(
        partial_value.reshape(expert_devices, local_experts * capacity, -1),
        "expert",
        split_axis=0,
        concat_axis=0,
        tiled=True,
    )
    width = returned.shape[-1]

    own = expert_ids.reshape(pair_count, 1) == jnp.arange(experts_all, dtype=jnp.int32)
    slot = jnp.sum(jnp.where(own, ranks(own), 0), 1)
    back_hit = own[:, :, None] & (slot[:, None, None] == cap_iota)
    gather_back = jnp.sum(
        back_hit.reshape(token_count, top_count, experts_all * capacity).astype(jnp.int32), 1
    ).astype(jnp.bfloat16)
    per_token = jnp.einsum(
        "tq,qd->td",
        gather_back,
        returned.reshape(experts_all * capacity, width),
        preferred_element_type=jnp.float32,
    )
    grad_tokens = lax.psum_scatter(per_token, "edata", scatter_dimension=1, tiled=True).astype(
        jnp.bfloat16
    )
    return (grad_tokens, grad_gate, grad_up, grad_down)


def dense_kernel(
    tokens_ref, dy_ref, ids_ref, prob_ref, wg_ref, wu_ref, wd_ref,
    gt_ref, gw_ref,
    act, wv, gh, gT, RC, RX, RY, RZ, pt,
    w_sem, own_sem, pt_s, pt_r, up_s, dn_s, col_r, edge_s, edge_r, tx_s, tx_r, ty_s, ty_r,
    gx_s, gx_r, gy_s, gy_r, hx_s, hx_r, hy_s, hy_r, gc_s, gc_r, rc_s, rc_r, rx_s, rx_r, ry_s, ry_r,
    rz_s, rz_r,
):
    T, FC = tokens_ref.shape
    H = wg_ref.shape[1]
    half = T // 2
    z = lax.axis_index("edata")
    p = lax.axis_index("expert")
    c = lax.rem(p, 2)
    x = lax.rem(lax.div(p, 2), 2)
    y = lax.div(p, 4)

    def q_of(qi):
        a, b = qi % 2, qi // 2
        if not isinstance(qi, int):
            a, b = lax.rem(qi, 2), lax.div(qi, 2)
        return (y + b * (1 - 2 * y)) * 2 + (x + a * (1 - 2 * x))

    def block_of(qi):
        return q_of(qi) * 2 + c

    px, py, pd, pc = block_of(1), block_of(2), block_of(3), q_of(0) * 2 + 1 - c
    dev_x, dev_y, dev_c = (z, px), (z, py), (z, pc)

    def rows(block, first=0, size=T):
        return pl.ds(pl.multiple_of(block * T + first, half), size)

    def cols(q):
        return pl.ds(pl.multiple_of(q * 2 * T, 2 * T), 2 * T)

    def feature_of(j):
        hi = lax.div(z, 2)
        zz = hi * (3 - z) + (1 - hi) * z
        near = jnp.where(j == 0, zz, 1 - zz)
        g = jnp.where(j < 2, near, j)
        return hi * (3 - g) + (1 - hi) * g

    def send(src, dst, s_sem, r_sem, dev):
        pltpu.make_async_remote_copy(
            src_ref=src, dst_ref=dst, send_sem=s_sem, recv_sem=r_sem,
            device_id=dev, device_id_type=MESH,
        ).start()

    def got(dst, sem):
        pltpu.make_async_copy(dst, dst, sem).wait()

    bar = pltpu.get_barrier_semaphore()
    for d in range(1, 8):
        pl.semaphore_signal(bar, inc=1, device_id=(z, lax.rem(p + d, 8)), device_id_type=MESH)
    for d in range(1, 4):
        pl.semaphore_signal(bar, inc=1, device_id=(lax.rem(z + d, 4), p), device_id_type=MESH)
    own_x = pltpu.make_async_copy(tokens_ref, act.at[0, z, rows(p)], own_sem.at[0])
    own_dy = pltpu.make_async_copy(dy_ref, act.at[1, z, rows(p)], own_sem.at[1])
    own_x.start()
    own_dy.start()
    wrefs = (wg_ref, wu_ref, wd_ref)

    def w_copy(r, j):
        f = feature_of(j)
        return pltpu.make_async_copy(
            wrefs[r // 2].at[r % 2, :, pl.ds(pl.multiple_of(f * FC, FC), FC)],
            wv.at[f, pl.ds(r * H, H), :],
            w_sem.at[r, j],
        )

    def weights_and_routing():
        for j in range(4):
            for r in range(6):
                w_copy(r, j).start()
        ids, prob = ids_ref[...], prob_ref[...]
        pt[p] = jnp.concatenate(
            [
                jnp.sum(jnp.where(ids == e, prob, 0.0), axis=0, keepdims=True)
                for e in range(pt.shape[1])
            ],
            axis=0,
        )
        for d in range(1, 8):
            send(pt.at[p], pt.at[p], pt_s.at[d - 1], pt_r.at[d - 1], (z, lax.rem(p + d, 8)))

    pl.semaphore_wait(bar, 10)

    def chain(ref, i, f):
        i = i * 4 + f

        @pl.when((f <= z) & (z < 3))
        def _():
            send(ref, ref, up_s.at[i], col_r.at[i], (z + 1, p))

        @pl.when((f >= z) & (z > 0))
        def _():
            send(ref, ref, dn_s.at[i], col_r.at[i], (z - 1, p))

    def tok_own(j):
        f = feature_of(j)
        ref = act.at[0, f, rows(p)]
        lo, hi = act.at[0, f, rows(p, 0, half)], act.at[0, f, rows(p, half, half)]

        @pl.when(j == 0)
        def _():
            own_x.wait()

        @pl.when(j > 0)
        def _():
            got(ref, col_r.at[f])

        chain(ref, 0, f)

        @pl.when(j == 0)
        def _():
            send(lo, lo, edge_s.at[0], edge_r.at[0], dev_x)
            send(hi, hi, edge_s.at[1], edge_r.at[1], dev_y)

    def tok_spread(j):
        f = feature_of(j)
        ref = act.at[0, f, rows(p)]
        lo, hi = act.at[0, f, rows(p, 0, half)], act.at[0, f, rows(p, half, half)]
        send(hi, hi, tx_s.at[0, j], tx_r.at[0, j], dev_x)
        send(lo, lo, ty_s.at[0, j], ty_r.at[0, j], dev_y)
        send(ref, ref, gc_s.at[0, j], gc_r.at[0, j], dev_c)

    def tok_edge(i, j):
        f = feature_of(j)
        block, first = (py, half) if i else (px, 0)
        ref = act.at[0, f, rows(block, first, half)]

        @pl.when(j == 0)
        def _():
            got(ref, edge_r.at[i])

        @pl.when(j > 0)
        def _():
            got(ref, col_r.at[8 + 4 * i + f])

        chain(ref, 2 + i, f)
        if i:
            send(ref, ref, tx_s.at[1, j], tx_r.at[1, j], dev_x)
        else:
            send(ref, ref, ty_s.at[1, j], ty_r.at[1, j], dev_y)

    def tok_near(i, j):
        f = feature_of(j)
        block, first, sem = (py, 0, ty_r) if i else (px, half, tx_r)
        got(act.at[0, f, rows(block, first, half)], sem.at[0, j])
        ref = act.at[0, f, rows(block)]
        send(ref, ref, gc_s.at[1 + i, j], gc_r.at[1 + i, j], dev_c)

    def tok_far(j):
        f = feature_of(j)
        got(act.at[0, f, rows(pd, half, half)], tx_r.at[1, j])
        got(act.at[0, f, rows(pd, 0, half)], ty_r.at[1, j])
        ref = act.at[0, f, rows(pd)]
        send(ref, ref, gc_s.at[3, j], gc_r.at[3, j], dev_c)

    def cot_own(j):
        f = feature_of(j)
        ref = act.at[1, f, rows(p)]

        @pl.when(j == 0)
        def _():
            own_dy.wait()

        @pl.when(j > 0)
        def _():
            got(ref, col_r.at[4 + f])

        chain(ref, 1, f)

    def cot_spread(j):
        ref = act.at[1, feature_of(j), rows(p)]
        send(ref, ref, gx_s.at[j], gx_r.at[j], dev_x)
        send(ref, ref, gy_s.at[j], gy_r.at[j], dev_y)
        send(ref, ref, gc_s.at[0, 4 + j], gc_r.at[0, 4 + j], dev_c)

    def cot_near(i, j):
        f = feature_of(j)
        block, sem = (py, gy_r) if i else (px, gx_r)
        ref = act.at[1, f, rows(block)]
        got(ref, sem.at[j])
        if i:
            on = act.at[1, f, rows(block, half, half)]
            send(on, on, hx_s.at[j], hx_r.at[j], dev_x)
        else:
            on = act.at[1, f, rows(block, 0, half)]
            send(on, on, hy_s.at[j], hy_r.at[j], dev_y)
        send(ref, ref, gc_s.at[1 + i, 4 + j], gc_r.at[1 + i, 4 + j], dev_c)

    def cot_far(j):
        f = feature_of(j)
        got(act.at[1, f, rows(pd, 0, half)], hy_r.at[j])
        got(act.at[1, f, rows(pd, half, half)], hx_r.at[j])
        ref = act.at[1, f, rows(pd)]
        send(ref, ref, gc_s.at[3, 4 + j], gc_r.at[3, 4 + j], dev_c)

    ET = 64

    def after_x(qi):
        q = q_of(qi)

        @pl.loop(0, 2 * H // ET)
        def _(n):
            e = lax.div(n, H // ET)
            prow = jnp.concatenate(
                [pt[2 * q, pl.ds(2 * p + e, 1), :], pt[2 * q + 1, pl.ds(2 * p + e, 1), :]], axis=1
            )
            a = pl.ds(pl.multiple_of(n * ET, ET), ET)
            b = pl.ds(pl.multiple_of(2 * H + n * ET, ET), ET)
            g, u = acc[qi, a, :], acc[qi, b, :]
            s = jax.nn.sigmoid(g)
            active = g * s
            gh[pl.ds(pl.multiple_of(4 * H + n * ET, ET), ET), cols(q)] = (
                active * u * prow
            ).astype(BF16)
            acc[qi, a, :] = u * s * (1.0 + g * (1.0 - s)) * prow
            acc[qi, b, :] = active * prow

    def after_dy(qi):
        q = q_of(qi)

        @pl.loop(0, 2)
        def _(e):
            for kind in range(2):
                lo = kind * 2 * H
                back = acc[qi, pl.ds(pl.multiple_of(4 * H + e * H, H), H), :]
                at = pl.ds(pl.multiple_of(lo + e * H, H), H)
                v = back * acc[qi, at, :]
                gh[at, cols(q)] = v.astype(BF16)
                gT[qi, :, at] = v.T.astype(BF16)

    def forward(arr, qi, j):
        f, q = feature_of(j), q_of(qi)
        got(act.at[arr, f, rows(q * 2 + 1 - c)], gc_r.at[qi, arr * 4 + j])
        if isinstance(qi, int) and qi == 0:
            for r in (4, 5) if arr else range(4):
                w_copy(r, j).wait()
            if not arr:

                @pl.when(j == 3)
                def _():
                    for d in range(1, 8):
                        got(pt.at[lax.rem(p + 8 - d, 8)], pt_r.at[d - 1])

        @pl.loop(2 * arr, 2 + arr)
        def _(n):
            at = pl.ds(pl.multiple_of(n * 2 * H, 2 * H), 2 * H)
            d = lax.dot_general(
                wv[f, at, :], act[arr, f, cols(q), :], (((1,), (1,)), ((), ())),
                preferred_element_type=F32,
            )

            @pl.when(j == 0)
            def _():
                acc[qi, at, :] = d

            @pl.when(j > 0)
            def _():
                acc[qi, at, :] += d

        @pl.when(j == 3)
        def _():
            if arr:
                after_dy(qi)
            else:
                after_x(qi)

    def both_near(arr, j):
        @pl.loop(1, 3)
        def _(qi):
            forward(arr, qi, j)

    gather_steps = (
        (4, lambda j: forward(1, 3, j)),
        (0, tok_own),
        (0, tok_spread),
        (0, lambda j: pl.when(j == 0)(weights_and_routing)),
        (2, lambda j: forward(0, 1, j)),
        (0, lambda j: forward(0, 0, j)),
        (2, lambda j: cot_near(1, j)),
        (1, lambda j: forward(1, 0, j)),
        (3, lambda j: forward(1, 1, j)),
        (1, lambda j: tok_edge(1, j)),
        (2, lambda j: cot_near(0, j)),
        (1, lambda j: tok_near(1, j)),
        (3, cot_far),
        (3, lambda j: forward(0, 3, j)),
        (2, lambda j: forward(1, 2, j)),
        (2, tok_far),
        (1, lambda j: tok_edge(0, j)),
        (0, cot_own),
        (1, lambda j: tok_near(0, j)),
        (0, cot_spread),
        (1, lambda j: forward(0, 2, j)),
    )

    def run(steps, u):
        for lag, step in steps:
            @pl.when((u >= lag) & (u < lag + 4))
            def _():
                step(u - lag)

    def gather(buf):
        nonlocal acc
        acc = buf

        @pl.loop(0, 8)
        def _(u):
            run(gather_steps, u)

    acc = Q = None
    pl.run_scoped(gather, pltpu.VMEM((4, 6 * H, 2 * T), F32))

    def quarter_of(k):
        m = 3 - k
        z0, z1 = lax.rem(z, 2), lax.div(z, 2)
        m0, m1 = lax.rem(m, 2), lax.div(m, 2)
        return (z0 + m0 * (1 - 2 * z0)) + 2 * (z1 + m1 * (1 - 2 * z1))

    def part(qi, k):
        f, q = quarter_of(k), q_of(qi)
        Q[f, cols(q), :] = jnp.dot(
            gT[qi], wv[f, pl.ds(0, 4 * H), :], preferred_element_type=F32
        ).astype(BF16)
        send(
            Q.at[f, rows(q * 2 + 1 - c)], RC.at[k, qi],
            rc_s.at[k, qi], rc_r.at[k, qi], dev_c,
        )

    AT = 32

    def add(dst, size, *terms):
        @pl.loop(0, size // AT)
        def _(n):
            at = pl.ds(pl.multiple_of(n * AT, AT), AT)
            total = dst[at, :].astype(F32)
            for t in terms:
                total = total + t[at, :].astype(F32)
            dst[at, :] = total.astype(BF16)

    def core_sum(qi, k):
        f = quarter_of(k)
        got(RC.at[k, qi], rc_r.at[k, qi])
        add(Q.at[f, rows(block_of(qi))], T, RC.at[k, qi])
        lo = Q.at[f, rows(block_of(qi), 0, half)]
        hi = Q.at[f, rows(block_of(qi), half, half)]
        if qi == 1:
            send(lo, RX.at[0, k], rx_s.at[0, k], rx_r.at[0, k], dev_x)
        elif qi == 2:
            send(hi, RY.at[0, k], ry_s.at[0, k], ry_r.at[0, k], dev_y)
        elif qi == 3:
            send(lo, RX.at[1, k], rx_s.at[1, k], rx_r.at[1, k], dev_x)
            send(hi, RY.at[1, k], ry_s.at[1, k], ry_r.at[1, k], dev_y)

    def turn_sums(k):
        f = quarter_of(k)
        got(RX.at[1, k], rx_r.at[1, k])
        lo = Q.at[f, rows(py, 0, half)]
        add(lo, half, RX.at[1, k])
        send(lo, RY.at[2, k], ry_s.at[2, k], ry_r.at[2, k], dev_y)
        got(RY.at[1, k], ry_r.at[1, k])
        hi = Q.at[f, rows(px, half, half)]
        add(hi, half, RY.at[1, k])
        send(hi, RX.at[2, k], rx_s.at[2, k], rx_r.at[2, k], dev_x)

    def plane_sums(k):
        f = quarter_of(k)
        got(RX.at[0, k], rx_r.at[0, k])
        got(RY.at[2, k], ry_r.at[2, k])
        add(Q.at[f, rows(p, 0, half)], half, RX.at[0, k], RY.at[2, k])
        got(RY.at[0, k], ry_r.at[0, k])
        got(RX.at[2, k], rx_r.at[2, k])
        add(Q.at[f, rows(p, half, half)], half, RY.at[0, k], RX.at[2, k])

        @pl.when(k < 3)
        def _():
            i = 2 - k
            send(Q.at[f, rows(p)], RZ.at[i], rz_s.at[i], rz_r.at[i], (f, p))

    def weight_grad(t):
        f, r = lax.div(t, 6), lax.rem(t, 6)
        gw_ref[r, :, pl.ds(pl.multiple_of(f * FC, FC), FC)] = jnp.dot(
            gh[pl.ds(pl.multiple_of(r * H, H), H), :], act[lax.div(r, 4), f],
            preferred_element_type=F32,
        ).astype(BF16)

    return_steps = (
        (0, lambda k: part(3, k)),
        (1, turn_sums),
        (0, lambda k: part(2, k)),
        (0, lambda k: part(1, k)),
        (0, lambda k: core_sum(3, k)),
        (1, lambda k: core_sum(0, k)),
    )
    more_return_steps = (
        (0, lambda k: core_sum(2, k)),
        (0, lambda k: core_sum(1, k)),
    )
    last_return_steps = (
        (1, plane_sums),
        (0, lambda k: part(0, k)),
    )

    def gather_sent():
        for d in range(1, 8):
            got(pt.at[p], pt_s.at[d - 1])

        def sent_along(i, f):
            ref = act.at[0, f, rows(p)] if i < 2 else act.at[0, f, rows(p, 0, half)]

            @pl.when((f <= z) & (z < 3))
            def _():
                got(ref, up_s.at[i * 4 + f])

            @pl.when((f >= z) & (z > 0))
            def _():
                got(ref, dn_s.at[i * 4 + f])

        part_ref = act.at[0, 0, rows(p, 0, half)]
        got(part_ref, edge_s.at[0])
        got(part_ref, edge_s.at[1])

        @pl.loop(0, 4)
        def _(j):
            for i in range(4):
                sent_along(i, j)
            for i in range(2):
                got(part_ref, tx_s.at[i, j])
                got(part_ref, ty_s.at[i, j])
            ref = act.at[0, 0, rows(p)]
            got(ref, gx_s.at[j])
            got(ref, gy_s.at[j])
            got(part_ref, hx_s.at[j])
            got(part_ref, hy_s.at[j])
            for i in range(4):
                got(ref, gc_s.at[i, j])
                got(ref, gc_s.at[i, 4 + j])

        @pl.loop(0, 4)
        def _(k):
            for qi in range(4):
                got(RC.at[k, qi], rc_s.at[k, qi])

    def sums_sent(k):
        for i in range(3):
            got(RX.at[i, k], rx_s.at[i, k])
            got(RY.at[i, k], ry_s.at[i, k])

    def give_back(buf):
        nonlocal Q
        Q = buf

        @pl.loop(0, 5)
        def _(u):
            @pl.when(u == 4)
            def _():
                gather_sent()
                for k in range(3):
                    sums_sent(k)

            run(return_steps, u)

            @pl.loop(0, 2)
            def _(n):
                weight_grad(u * 5 + n)

            run(more_return_steps, u)

            @pl.loop(2, 5 - lax.div(u, 4))
            def _(n):
                weight_grad(u * 5 + n)

            run(last_return_steps, u)

        sums_sent(3)
        for i in range(3):
            got(RZ.at[i], rz_r.at[i])

        @pl.loop(0, T // AT)
        def _(n):
            at = pl.ds(pl.multiple_of(n * AT, AT), AT)
            total = Q[z, pl.ds(pl.multiple_of(p * T + n * AT, AT), AT), :].astype(F32)
            for i in range(3):
                total = total + RZ[i, at, :].astype(F32)
            gt_ref[at, :] = total.astype(BF16)

        for i in range(3):
            got(RZ.at[i], rz_s.at[i])

    pl.run_scoped(give_back, pltpu.VMEM((4, act.shape[2], FC), BF16))


def to_hbm_kernel(gt_ref, gw_ref, gt_out, gate_out, up_out, down_out, sem):
    copies = [pltpu.make_async_copy(gt_ref, gt_out, sem.at[6])]
    for r in range(6):
        out = (gate_out, up_out, down_out)[r // 2]
        copies.append(pltpu.make_async_copy(gw_ref.at[r], out.at[r % 2], sem.at[r]))
    for c in copies:
        c.start()
    for c in copies:
        c.wait()


def dense_body(tokens, grad_out, expert_ids, route_prob, w_gate, w_up, w_down):
    T, FC = tokens.shape
    E, H, D = w_gate.shape
    blocks = lax.axis_size("expert")
    N = blocks * T
    experts = blocks * E
    dma = pltpu.SemaphoreType.DMA
    any_ = pl.BlockSpec(memory_space=pl.ANY)
    vmem = pl.BlockSpec(memory_space=pltpu.VMEM)
    grad_tokens, gw = pl.pallas_call(
        dense_kernel,
        out_shape=(pltpu.VMEM((T, FC), BF16), pltpu.VMEM((3 * E, H, D), BF16)),
        in_specs=[any_, any_, vmem, vmem, any_, any_, any_],
        out_specs=(vmem, vmem),
        scratch_shapes=[
            pltpu.VMEM((2, 4, N, FC), BF16),
            pltpu.VMEM((4, 6 * H, FC), BF16),
            pltpu.VMEM((6 * H, N), BF16),
            pltpu.VMEM((4, 2 * T, 4 * H), BF16),
            pltpu.VMEM((4, 4, T, FC), BF16),
            pltpu.VMEM((3, 4, T // 2, FC), BF16),
            pltpu.VMEM((3, 4, T // 2, FC), BF16),
            pltpu.VMEM((3, T, FC), BF16),
            pltpu.VMEM((blocks, experts, 128), F32),
            dma((6, 4)), dma((2,)), dma((7,)), dma((7,)),
            dma((16,)), dma((16,)), dma((16,)), dma((2,)), dma((2,)),
            dma((2, 4)), dma((2, 4)), dma((2, 4)), dma((2, 4)),
            dma((4,)), dma((4,)), dma((4,)), dma((4,)),
            dma((4,)), dma((4,)), dma((4,)), dma((4,)),
            dma((4, 8)), dma((4, 8)), dma((4, 4)), dma((4, 4)),
            dma((3, 4)), dma((3, 4)), dma((3, 4)), dma((3, 4)),
            dma((3,)), dma((3,)),
        ],
        compiler_params=pltpu.CompilerParams(
            collective_id=0, has_side_effects=True, vmem_limit_bytes=51 << 20
        ),
        cost_estimate=pl.CostEstimate(
            flops=2 * N * D * 16 * H, bytes_accessed=12 * E * H * D, transcendentals=N * E * H
        ),
    )(tokens, grad_out, expert_ids.T, route_prob.T, w_gate, w_up, w_down)
    grad_w = jax.ShapeDtypeStruct((E, H, D), BF16)
    return pl.pallas_call(
        to_hbm_kernel,
        out_shape=(jax.ShapeDtypeStruct((T, FC), BF16), grad_w, grad_w, grad_w),
        in_specs=[any_, any_],
        out_specs=(any_,) * 4,
        scratch_shapes=[dma((7,))],
        compiler_params=pltpu.CompilerParams(vmem_limit_bytes=1 << 20),
    )(grad_tokens, gw)


def solution(mesh):
    placed = (
        P("expert", "edata"),
        P("expert", "edata"),
        P("expert", None),
        P("expert", None),
        P("expert", "edata", None),
        P("expert", "edata", None),
        P("expert", "edata", None),
    )
    small = mesh.shape["expert"] == 8 and mesh.shape["edata"] == 4
    return jax.shard_map(
        dense_body if small else slots_body,
        mesh=mesh,
        in_specs=placed,
        out_specs=(
            P("expert", "edata"),
            P("expert", "edata", None),
            P("expert", "edata", None),
            P("expert", "edata", None),
        ),
        check_vma=False,
    )
```
